512 devices in a mesh: gx: 8 (over z_hi, core), gy: 8 (over y), gz: 8 (over x, z_lo).
Axes of the slice: x: 4, y: 8, z: 8 (z_hi: 4, z_lo: 2; z = z_hi * 2 + z_lo), core: 2. Of those that a mesh axis runs over, the one named last changes fastest.
Arguments:
- features: bfloat16 [8, 8, 8, 128, 128], P('gx', 'gy', 'gz'), may hold values from -6 to 6
- positions: float32 [8, 8, 8, 3, 128], P('gx', 'gy', 'gz'), may hold values from 0 to 1
- counts: int32 [8, 8, 8], P('gx', 'gy', 'gz'), may hold values from 1 to 128, as said below
- w_proj: bfloat16 [4, 128, 128], replicated, may hold values from -0.5 to 0.5
- w_mix: bfloat16 [128, 128], replicated, may hold values from -0.5 to 0.5
- w_long: bfloat16 [64, 128], replicated, may hold values from -0.75 to 0.75
- w_charge: bfloat16 [64, 128], replicated, may hold values from -0.5 to 0.5
- charge_bias: float32 [64], replicated, may hold values from -4 to 4
- w_energy: float32 [128], replicated, may hold values from -0.5 to 0.5
- k_filter: float32 [64, 2048], replicated, may hold values from 0.1 to 1
- k_index: int32 [3, 2048], replicated, may hold values from -6 to 6
Outputs:
- updated: bfloat16 [8, 8, 8, 128, 128], P('gx', 'gy', 'gz')
- energies: float32 [8, 8, 8, 128], P('gx', 'gy', 'gz')
- forces: float32 [8, 8, 8, 3, 128], P('gx', 'gy', 'gz')
The draws below stay inside these ranges and needn't reach their ends.
Inputs may be any that keep to these rules, and one draw needn't show every extreme that they name: Slots 0 to counts[x,y,z] - 1 of cell (x,y,z) hold live atoms, the rest are padding; some cell holds 128 live atoms.
All inputs are finite; a program needn't handle non-finite values.
Results may differ from the reference program's by a relative error of at most 0.0068.
Values may be sent and summed in bfloat16 or wider, within the bound.
A program may use at most 64 MiB of HBM per device.

```python
import math
import jax
import jax.numpy as jnp
from jax import lax

CHANNELS = 128
BASES = 4
CHARGE_CH = 64
WAVES = 2048
ATOMS_CELL = 128
CELLS_X = 8
CELLS_Y = 8
CELLS_Z = 8


def draw_counts(key, part):
    levels = jnp.arange(CELLS_X, dtype=jnp.int32)
    lowest = ATOMS_CELL // 3
    rising = lowest + (ATOMS_CELL - lowest) * levels // max(CELLS_X - 1, 1)
    jitter = jax.random.randint(jax.random.fold_in(key, 11), (CELLS_X, CELLS_Y, CELLS_Z), 0, ATOMS_CELL // 8 + 1)
    counted = jnp.maximum(rising[:, None, None] - jitter, 1)
    counted = counted.at[CELLS_X - 1, 0, 0].set(ATOMS_CELL)
    return counted.astype(jnp.int32)


def with_ends(entries, stream_key, low, top_value):
    dims = entries.shape
    index_at = [jax.random.randint(jax.random.fold_in(stream_key, axis), (), 0, dims[axis]) for axis in range(len(dims))]
    entries = entries.at[tuple(index_at)].set(low)
    longest = dims.index(max(dims))
    index_at[longest] = (index_at[longest] + 1) % dims[longest]
    return entries.at[tuple(index_at)].set(top_value)


def block_levels(own_key, shape, pieces, low, top_value):
    loudness = 1.0
    for axis_at, blocks in pieces:
        draws = jax.random.uniform(jax.random.fold_in(jax.random.fold_in(own_key, 6), axis_at), (blocks,), jnp.float32, low / len(pieces), top_value / len(pieces))
        loudness = loudness * jnp.repeat(jnp.exp(draws), shape[axis_at] // blocks).reshape((-1,) + (1,) * (len(shape) - 1 - axis_at))
    return loudness


def noise(own_key, dims, deviation, reach, cuts=(), held_as=jnp.bfloat16):
    result = jax.random.normal(own_key, dims, jnp.float32) * deviation
    if len(cuts) > 0:
        result = block_levels(own_key, dims, cuts, -0.22, 0.18) * result
    return jnp.clip(result, min=-reach, max=reach).astype(held_as)


def setup_inputs(seed: int = 0) -> dict:
    key_of = jax.random.split(jax.random.key(seed), 12)
    return {
        "features": noise(key_of[0], (CELLS_X, CELLS_Y, CELLS_Z, ATOMS_CELL, CHANNELS), 1.0, 6.0, ((0, 8), (1, 8), (2, 8))),
        "positions": jnp.clip(1.0 * jax.random.uniform(key_of[1], (CELLS_X, CELLS_Y, CELLS_Z, 3, ATOMS_CELL), jnp.float32) ** block_levels(key_of[1], (CELLS_X, CELLS_Y, CELLS_Z, 3, ATOMS_CELL), ((0, 8), (1, 8), (2, 8)), -0.2, 0.2), 0.0, 1.0),
        "counts": draw_counts(jax.random.fold_in(key_of[11], 71), 0),
        "w_proj": noise(key_of[3], (BASES, CHANNELS, CHANNELS), CHANNELS ** -0.5, 0.5),
        "w_mix": noise(key_of[4], (CHANNELS, CHANNELS), CHANNELS ** -0.5, 0.5),
        "w_long": noise(key_of[5], (CHARGE_CH, CHANNELS), CHARGE_CH ** -0.5, 0.75),
        "w_charge": noise(key_of[6], (CHARGE_CH, CHANNELS), CHANNELS ** -0.5, 0.5),
        "charge_bias": noise(key_of[7], (CHARGE_CH,), 1.0, 4.0, (), jnp.float32),
        "w_energy": noise(key_of[8], (CHANNELS,), CHANNELS ** -0.5, 0.5, (), jnp.float32),
        "k_filter": jnp.clip(jnp.exp(jax.random.uniform(key_of[9], (CHARGE_CH, WAVES), jnp.float32, math.log(0.1), math.log(1.0))), 0.1, 1.0),
        "k_index": with_ends(jax.random.randint(key_of[10], (3, WAVES), -6, 7), jax.random.fold_in(key_of[10], 1), -6, 6).astype(jnp.int32),
    }


CUTOFF = 0.9
GAMMAS = (1.0, 3.0, 8.0, 20.0)
PRECISE = lax.Precision.HIGHEST
CONTRACT_LAST = (((1,), (1,)), ((), ()))
CONTRACT_FIRST = (((0,), (0,)), ((), ()))

def silu_grad(values):
    sigma = jax.nn.sigmoid(values)
    return sigma * (1.0 + values * (1.0 - sigma))

def pair_geometry(centre, others, neighbour):
    cell_shift = jnp.stack([neighbour // 9, neighbour // 3 % 3, neighbour % 3]).astype(jnp.float32) - 1.0
    offset_vec = others[:, None, :] + cell_shift[:, None, None] - centre[:, :, None]
    scaled = lax.optimization_barrier(jnp.sum(offset_vec * offset_vec, axis=0)) / (CUTOFF * CUTOFF)
    atom_count = centre.shape[1]
    slot_ids = jnp.arange(atom_count, dtype=jnp.int32)
    self_pair = (slot_ids[:, None] == slot_ids[None, :]) & (neighbour == 13)
    keep_mask = jnp.where(self_pair, 0.0, 1.0).astype(jnp.float32)
    envelope_base = jnp.maximum(1.0 - scaled, 0.0)
    decay_rates = jnp.asarray(GAMMAS, dtype=jnp.float32)[None, :, None]
    decay_terms = jnp.exp(-decay_rates * scaled[:, None, :]) * keep_mask[:, None, :]
    envelope = (envelope_base * envelope_base)[:, None, :]
    radial = decay_terms * envelope
    radial_slope = decay_terms * (-decay_rates * envelope - 2.0 * envelope_base[:, None, :])
    return (offset_vec, radial, radial_slope)

def phases(absolute, wave_vec):
    phase_angle = absolute[0][:, None] * wave_vec[0][None, :] + absolute[1][:, None] * wave_vec[1][None, :] + absolute[2][:, None] * wave_vec[2][None, :]
    return (jnp.cos(phase_angle), jnp.sin(phase_angle))

def reference(features, positions, counts, w_proj, w_mix, w_long, w_charge, charge_bias, w_energy, k_filter, k_index):
    cells_first, cells_second, cells_third = (features.shape[0], features.shape[1], features.shape[2])
    atom_count = features.shape[3]
    channels = features.shape[4]
    basis_count = w_proj.shape[0]
    cell_total = cells_first * cells_second * cells_third
    waves = k_index.shape[1]
    scale_long = 4.0 / math.sqrt(atom_count * cell_total * waves)
    living = (jnp.arange(atom_count, dtype=jnp.int32)[None, None, None, :] < counts[:, :, :, None]).astype(jnp.float32)
    masked = features * living[..., None].astype(jnp.bfloat16)
    basis_values = jnp.einsum('xyzjc,bcd->xyzbjd', masked.astype(jnp.float32), w_proj.astype(jnp.float32)).astype(jnp.bfloat16)
    charges = jax.nn.silu(jnp.einsum('ec,xyzjc->xyzej', w_charge.astype(jnp.float32), masked.astype(jnp.float32)) + charge_bias[:, None]) * living[:, :, :, None, :]
    charge_mean = lax.optimization_barrier(jnp.sum(charges, axis=(0, 1, 2, 4))) / jnp.sum(living)
    neutral = (charges - charge_mean[:, None]) * living[:, :, :, None, :]
    extent = jnp.asarray([cells_first, cells_second, cells_third], dtype=jnp.float32)
    wave_vec = 2.0 * math.pi * k_index.astype(jnp.float32) / extent[:, None]
    grid_x = jnp.arange(cells_first, dtype=jnp.int32)[:, None, None] + 0 * jnp.arange(cells_second, dtype=jnp.int32)[None, :, None] + 0 * jnp.arange(cells_third, dtype=jnp.int32)[None, None, :]
    grid_y = 0 * grid_x + jnp.arange(cells_second, dtype=jnp.int32)[None, :, None]
    grid_z = 0 * grid_x + jnp.arange(cells_third, dtype=jnp.int32)[None, None, :]
    anchor = jnp.stack([grid_x, grid_y, grid_z], axis=3).astype(jnp.float32)
    absolute = positions + anchor[..., None]
    flat_abs = absolute.reshape(cell_total, 3, atom_count)
    flat_neutral = neutral.reshape(cell_total, neutral.shape[3], atom_count)
    empty = jnp.zeros((neutral.shape[3], waves), jnp.float32)

    def add_structure(carry, item):
        place, charge_rows = item
        cosine, sine_part = phases(place, wave_vec)
        return ((carry[0] + jnp.dot(charge_rows, cosine, precision=PRECISE), carry[1] + jnp.dot(charge_rows, sine_part, precision=PRECISE)), None)
    (struct_c, struct_s), _ = lax.scan(add_structure, (empty, empty), (flat_abs, flat_neutral))
    filtered_cos = k_filter * struct_c
    filtered_sin = k_filter * struct_s

    def locate(cell_id, neighbour):
        cell_x = cell_id // (cells_second * cells_third)
        cell_y = cell_id // cells_third % cells_second
        cell_z = cell_id % cells_third
        return ((cell_x + neighbour // 9 - 1) % cells_first, (cell_y + neighbour // 3 % 3 - 1) % cells_second, (cell_z + neighbour % 3 - 1) % cells_third)

    def forward_cell(carry, cell_id):
        home = locate(cell_id, 13)
        own_rows = features[home]
        centre = positions[home]
        alive_row = living[home]
        message = jnp.zeros((atom_count, channels), jnp.float32)
        for neighbour in range(27):
            near_cell = locate(cell_id, neighbour)
            offset_vec, radial, radial_slope = pair_geometry(centre, positions[near_cell], neighbour)
            message = message + jnp.dot(radial.astype(jnp.bfloat16).reshape(atom_count, -1), basis_values[near_cell].reshape(-1, channels), preferred_element_type=jnp.float32)
        cosine, sine_part = phases(flat_abs[cell_id], wave_vec)
        potential = scale_long * (lax.dot_general(filtered_cos, cosine, CONTRACT_LAST, precision=PRECISE) + lax.dot_general(filtered_sin, sine_part, CONTRACT_LAST, precision=PRECISE))
        pre_act = jnp.dot(message.astype(jnp.bfloat16), w_mix, preferred_element_type=jnp.float32) + lax.dot_general(potential.astype(jnp.bfloat16), w_long, CONTRACT_FIRST, preferred_element_type=jnp.float32)
        refined = own_rows.astype(jnp.float32) + jax.nn.silu(pre_act)
        energy = alive_row * lax.optimization_barrier(jnp.sum(jax.nn.silu(refined) * w_energy[None, :], axis=1))
        grad_new = alive_row[:, None] * w_energy[None, :] * silu_grad(refined)
        grad_pre = (grad_new * silu_grad(pre_act)).astype(jnp.bfloat16)
        adjoint = lax.dot_general(grad_pre, w_mix, CONTRACT_LAST, preferred_element_type=jnp.float32).astype(jnp.bfloat16)
        pull_back = lax.dot_general(w_long, grad_pre, CONTRACT_LAST, preferred_element_type=jnp.float32)
        carry = (carry[0] + jnp.dot(pull_back, cosine, precision=PRECISE), carry[1] + jnp.dot(pull_back, sine_part, precision=PRECISE))
        return (carry, (refined.astype(jnp.bfloat16), energy, adjoint, pull_back))
    cell_ids = jnp.arange(cell_total, dtype=jnp.int32)
    (back_c, back_s), (updated, energies, adjoints, pulls) = lax.scan(forward_cell, (empty, empty), cell_ids)
    adjoint_grid = adjoints.reshape(cells_first, cells_second, cells_third, atom_count, channels)
    weights_along = jnp.concatenate([filtered_sin, k_filter * back_s], axis=0)
    weights_across = jnp.concatenate([filtered_cos, k_filter * back_c], axis=0)

    def force_cell(cell_id):
        home = locate(cell_id, 13)
        centre = positions[home]
        local_proj = basis_values[home]
        own_adjoint = adjoint_grid[home]
        near_force = jnp.zeros((3, atom_count), jnp.float32)
        for neighbour in range(27):
            near_cell = locate(cell_id, neighbour)
            offset_vec, radial, radial_slope = pair_geometry(centre, positions[near_cell], neighbour)
            first_term = lax.dot_general(own_adjoint, basis_values[near_cell].reshape(-1, channels), CONTRACT_LAST, preferred_element_type=jnp.float32).reshape(atom_count, basis_count, atom_count)
            second_term = jnp.einsum('bic,jc->ibj', local_proj.astype(jnp.float32), adjoint_grid[near_cell].astype(jnp.float32))
            strength = lax.optimization_barrier(jnp.sum(radial_slope * (first_term + second_term), axis=1))
            near_force = near_force + 2.0 / (CUTOFF * CUTOFF) * lax.optimization_barrier(jnp.sum(strength[None, :, :] * offset_vec, axis=2))
        cosine, sine_part = phases(flat_abs[cell_id], wave_vec)
        mixing = jnp.concatenate([pulls[cell_id], flat_neutral[cell_id]], axis=0)
        along_term = lax.dot_general(mixing, weights_along, CONTRACT_FIRST, precision=PRECISE)
        across_term = lax.dot_general(mixing, weights_across, CONTRACT_FIRST, precision=PRECISE)
        ewald_grad = lax.dot_general(wave_vec, cosine * along_term - sine_part * across_term, CONTRACT_LAST, precision=PRECISE)
        return near_force - scale_long * ewald_grad
    forces = lax.map(force_cell, cell_ids)
    return (updated.reshape(features.shape), energies.reshape(cells_first, cells_second, cells_third, atom_count), forces.reshape(positions.shape))
```

```python
import functools
import math

import jax
import jax.numpy as jnp
from jax import lax
from jax.experimental import pallas as pl
from jax.experimental.pallas import tpu as pltpu
from jax.sharding import PartitionSpec as P

MESH = pl.DeviceIdType.MESH
CUTOFF2 = 0.9 * 0.9
ATOMS = 128
CHANNELS = 128
BASES = 4
EDGE = 8
WAVES = 2048
TOP = 6
SIDE = 2 * TOP + 1
TILES = 8
ROWS = 192
CHUNK = 24
SLOTS = TILES * ROWS
F32 = jnp.float32
BF16 = jnp.bfloat16
NT = (((1,), (1,)), ((), ()))
NN = (((1,), (0,)), ((), ()))
TN = (((0,), (0,)), ((), ()))


def dot(a, b, dims=NN):
    return lax.dot_general(a, b, dims, preferred_element_type=F32)


def split(value):
    high = value.astype(BF16)
    low = (value - high.astype(F32)).astype(BF16)
    return high, low


def dot3(a_high, a_low, b_high, b_low, dims=NN):
    return dot(a_high, b_high, dims) + dot(a_high, b_low, dims) + dot(a_low, b_high, dims)


def iota(shape, dim):
    return lax.broadcasted_iota(jnp.int32, shape, dim)


def sigmoid(v):
    return 1.0 / (1.0 + jnp.exp(-v))


def block_kernel(
    counts_ref,
    feat_ref,
    pos_ref,
    wproj_ref,
    wmix_ref,
    wlong_ref,
    wcharge_ref,
    rows_ref,
    kf_ref,
    kidx_ref,
    upd_ref,
    energy_ref,
    force_ref,
    nfeat,
    nadj,
    npos,
    trig,
    wave_f,
    wave_h,
    wave_l,
    filt,
    fs_h,
    fs_l,
    part1,
    got1z,
    mid1,
    got1y,
    low1,
    got1x,
    up1,
    all1,
    part2,
    got2z,
    mid2,
    got2y,
    low2,
    got2x,
    up2,
    all2,
    tot0,
    tot1,
    tot2,
    gott,
    pcol,
    rad,
    wcat,
    nbasis,
    acc,
    prod,
    uv,
    pull,
    send_sem,
    recv_sem,
    tsend,
    trecv,
    hsend,
    hrecv,
):
    me = tuple(lax.axis_index(name) for name in ("gx", "gy", "gz"))

    def device_at(axis, distance):
        coords = list(me)
        coords[axis] = lax.rem(me[axis] + distance, EDGE)
        return coords[axis], tuple(coords)

    barrier = pltpu.get_barrier_semaphore()
    for axis in range(3):
        for d in range(1, EDGE):
            pl.semaphore_signal(
                barrier, inc=1, device_id=device_at(axis, d)[1], device_id_type=MESH
            )

    sent = []

    def send(src, dst, ssem, rsem, device):
        copy = pltpu.make_async_remote_copy(
            src_ref=src,
            dst_ref=dst,
            send_sem=ssem,
            recv_sem=rsem,
            device_id=device,
            device_id_type=MESH,
        )
        copy.start()
        sent.append(copy)
        return copy

    def spread(axis, stage, source, target):
        copies = []
        for d in range(1, EDGE):
            peer, device = device_at(axis, d)
            copies.append(
                send(
                    source(peer),
                    target(d - 1),
                    send_sem.at[stage, d - 1],
                    recv_sem.at[stage, d - 1],
                    device,
                )
            )
        return copies

    def arrive(copies):
        for copy in copies:
            copy.wait_recv()

    live_row = (iota((1, ATOMS), 1) < counts_ref[0]).astype(F32)
    live_col = (iota((ATOMS, CHANNELS), 0) < counts_ref[0]).astype(F32)
    own = feat_ref[...]
    masked = own * live_col.astype(BF16)
    nfeat[13] = masked
    npos[13] = jnp.zeros((8, ATOMS), F32)
    npos[13, 0:3, :] = pos_ref[...]

    wcharge2 = jnp.concatenate([wcharge_ref[...], wcharge_ref[...]], axis=0)
    charge_pre = dot(masked, wcharge2, NT) + rows_ref[0:1, :]
    charge = charge_pre * sigmoid(charge_pre) * live_col
    tot0[0:1, :] = jnp.sum(charge, axis=0, keepdims=True)
    tot0[1:8, :] = jnp.broadcast_to(jnp.sum(live_col, axis=0, keepdims=True), (7, ATOMS))

    steps = iota((8, ATOMS), 0).astype(F32)
    for axis in range(3):
        unit = (pos_ref[axis : axis + 1, :] + me[axis].astype(F32)) * (1.0 / EDGE)
        orders = steps if axis < 2 else jnp.where(steps > 6.5, 0.0, steps)
        turns = orders * unit
        angle = (turns - jnp.floor(turns + 0.5)) * (2.0 * math.pi)
        trig[2 * axis] = jnp.cos(angle)
        trig[2 * axis + 1] = jnp.sin(angle)
    z_c = trig[4]
    z_s = trig[5]
    y_c = [jnp.broadcast_to(trig[2, m : m + 1, :], (8, ATOMS)) for m in range(TOP + 1)]
    y_s = [jnp.broadcast_to(trig[3, m : m + 1, :], (8, ATOMS)) for m in range(TOP + 1)]

    def put_wave(group, c, s):
        tile, row = group // 24, (group % 24) * 8
        wave_f[tile, row : row + 8, 0:ATOMS] = c
        wave_f[tile, row : row + 8, ATOMS : 2 * ATOMS] = s

    for kx in range(-TOP, TOP + 1):
        x_c = trig[0, abs(kx) : abs(kx) + 1, :]
        x_s = trig[1, abs(kx) : abs(kx) + 1, :]
        if kx < 0:
            x_s = -x_s
        xz_c = x_c * z_c - x_s * z_s
        xz_s = x_c * z_s + x_s * z_c
        base = (kx + TOP) * SIDE + TOP
        put_wave(base, xz_c, xz_s)
        for ky in range(1, TOP + 1):
            cc, ss = xz_c * y_c[ky], xz_s * y_s[ky]
            cs, sc = xz_c * y_s[ky], xz_s * y_c[ky]
            put_wave(base + ky, cc - ss, cs + sc)
            put_wave(base - ky, cc + ss, sc - cs)
    for group in range(SIDE * SIDE, SLOTS // 8):
        put_wave(group, jnp.zeros((8, ATOMS), F32), jnp.zeros((8, ATOMS), F32))

    half = iota((ATOMS, ATOMS), 1) < 64
    q_h, q_l = split(
        jnp.concatenate([jnp.where(half, charge, 0.0), jnp.where(half, 0.0, charge)], axis=0)
    )
    acc[0:128, :] = jnp.zeros((128, 128), F32)
    acc[128:256, :] = jnp.zeros((128, 128), F32)
    acc[0:8, :] = z_c * live_row
    acc[64:72, :] = z_s * live_row
    acc[128:136, :] = -(z_s * live_row)
    acc[192:200, :] = z_c * live_row
    live_rhs = jnp.concatenate(
        [jnp.transpose(acc[0:128, :]), jnp.transpose(acc[128:256, :])], axis=0
    )
    l_h, l_l = split(live_rhs)
    both_h = jnp.concatenate([q_h, l_h], axis=1)
    both_l = jnp.concatenate([q_l, l_l], axis=1)
    spare = lax.rem(iota((ROWS, 128), 0), 8) == 7

    @pl.loop(0, TILES)
    def _(t):
        w_h, w_l = split(wave_f[t])
        wave_h[t] = w_h
        wave_l[t] = w_l
        sums = dot3(w_h, w_l, both_h, both_l)
        part1[t] = jnp.where(spare, sums[:, 128:256], sums[:, 0:128]).astype(BF16)

    pl.semaphore_wait(barrier, 3 * (EDGE - 1))

    def totals(axis, stage, source):
        copies = []
        for d in range(1, EDGE):
            copies.append(
                send(
                    source,
                    gott.at[stage, d - 1],
                    tsend.at[stage, d - 1],
                    trecv.at[stage, d - 1],
                    device_at(axis, d)[1],
                )
            )
        return copies

    def gathered_totals(copies, stage, source):
        arrive(copies)
        value = source[...]
        for d in range(1, EDGE):
            value = value + gott[stage, d - 1]
        return value

    def shift(axis, stage, kind, buffer, source, before, after, width):
        ring = []
        for side, distance in ((0, 1), (1, EDGE - 1)):
            start = before if side == 0 else after
            ring.append(
                send(
                    buffer.at[pl.ds(source, width)] if width > 1 else buffer.at[source],
                    buffer.at[pl.ds(start, width)] if width > 1 else buffer.at[start],
                    hsend.at[kind, stage, side],
                    hrecv.at[kind, stage, side],
                    device_at(axis, distance)[1],
                )
            )
        return ring

    def halo(stage, kind, buffer):
        if stage == 0:
            return shift(2, 0, kind, buffer, 13, 12, 14, 1)
        if stage == 1:
            return shift(0, 1, kind, buffer, 12, 9, 15, 3)
        return shift(1, 2, kind, buffer, 9, 0, 18, 9)

    red_z = spread(2, 0, lambda peer: part1.at[peer], lambda s: got1z.at[s])
    tot_z = totals(2, 0, tot0)
    halo_f = halo(0, 0, nfeat)
    halo_p = halo(0, 1, npos)

    k_h, k_l = split(kf_ref[...])
    kf2 = jnp.concatenate([k_h, k_l], axis=0)
    kx, ky, kz = kidx_ref[0:1, :], kidx_ref[1:2, :], kidx_ref[2:3, :]
    sign = jnp.where(kz < 0, -1, 1)
    slot = ((kx * sign + TOP) * SIDE + (ky * sign + TOP)) * 8 + kz * sign
    scale = 4.0 / math.sqrt(ATOMS * EDGE * EDGE * EDGE * WAVES)

    @pl.loop(0, TILES)
    def _(t):
        hot = jnp.where(iota((ROWS, WAVES), 0) + t * ROWS == slot, 1.0, 0.0).astype(BF16)
        part = dot(hot, kf2, NT)
        filt[t] = (part + pltpu.roll(part, 64, axis=1)) * scale

    for axis in range(3):
        pcol[axis] = jnp.transpose(jnp.broadcast_to(pos_ref[axis : axis + 1, :], (ATOMS, ATOMS)))
    acc[0:ATOMS, :] = jnp.zeros((ATOMS, CHANNELS), F32)
    for b in range(BASES):
        wcat[:, b * CHANNELS : b * CHANNELS + CHANNELS] = wproj_ref[b]

    def pair(q, oz, row0, rows):
        where = npos[q * 3 + oz]
        shift_y = (q // 3 - 1).astype(F32)
        shift_x = (lax.rem(q, 3) - 1).astype(F32)
        dx = (where[0:1, :] + shift_x) - pcol[0, row0 : row0 + rows, :]
        dy = (where[1:2, :] + shift_y) - pcol[1, row0 : row0 + rows, :]
        dz = (where[2:3, :] + float(oz - 1)) - pcol[2, row0 : row0 + rows, :]
        scaled = (dx * dx + dy * dy + dz * dz) * (1.0 / CUTOFF2)
        base = jnp.maximum(1.0 - scaled, 0.0)
        if oz == 1:
            same = iota((rows, ATOMS), 0) + row0 == iota((rows, ATOMS), 1)
            base = base * jnp.where(same, jnp.where(q == 4, 0.0, 1.0), 1.0)
        e1 = jnp.exp(-scaled)
        e2 = e1 * e1
        e3 = e2 * e1
        e4 = e2 * e2
        e8 = e4 * e4
        e20 = e8 * e8 * e4
        return dx, dy, dz, base, (e1, e3, e8, e20)

    STRIP = 32

    def message_block(q):
        for oz in range(3):
            for row0 in range(0, ATOMS, STRIP):
                _, _, _, base, decay = pair(q, oz, row0, STRIP)
                envelope = base * base
                for b in range(BASES):
                    column = (oz * BASES + b) * ATOMS
                    rad[row0 : row0 + STRIP, column : column + ATOMS] = (
                        decay[b] * envelope
                    ).astype(BF16)
            values = dot(nfeat[q * 3 + oz], wcat[...]).astype(BF16)
            for b in range(BASES):
                nbasis[q * 3 + oz, b * ATOMS : b * ATOMS + ATOMS, :] = values[
                    :, b * CHANNELS : b * CHANNELS + CHANNELS
                ]
        near = nbasis[pl.ds(q * 3, 3)].reshape(3 * BASES * ATOMS, CHANNELS)
        acc[0:ATOMS, :] += dot(rad[...], near)

    def reduced(own_part, got):
        value = own_part.astype(F32)
        for d in range(1, EDGE):
            value = value + got[d - 1].astype(F32)
        return value

    arrive(red_z)
    value = reduced(part1[me[2]], got1z)
    for c in range(EDGE):
        mid1[c] = value[c * CHUNK : c * CHUNK + CHUNK, :]
    red_y = spread(1, 1, lambda peer: mid1.at[peer], lambda s: got1y.at[s])
    tot1[...] = gathered_totals(tot_z, 0, tot0)
    tot_y = totals(1, 1, tot1)
    arrive(halo_f)
    arrive(halo_p)
    halo_f = halo(1, 0, nfeat)
    halo_p = halo(1, 1, npos)
    message_block(jnp.int32(4))

    arrive(red_y)
    low1[...] = reduced(mid1[me[1]], got1y)
    red_x = spread(0, 2, lambda peer: low1, lambda s: got1x.at[s])
    tot2[...] = gathered_totals(tot_y, 1, tot1)
    tot_x = totals(0, 2, tot2)
    arrive(halo_f)
    arrive(halo_p)
    halo_f = halo(2, 0, nfeat)
    halo_p = halo(2, 1, npos)
    message_block(jnp.int32(3))
    message_block(jnp.int32(5))

    arrive(red_x)
    value = reduced(low1[...], got1x)
    total = gathered_totals(tot_x, 2, tot2)
    mean = total[0:1, :] / total[1:2, :]
    lane8 = iota((8, 128), 1)
    row8 = iota((8, 128), 0)
    for g in range(CHUNK // 8):
        tile = value[g * 8 : g * 8 + 8, :]
        live = jnp.broadcast_to(tile[7:8, :], (8, 128))
        live_c = jnp.sum(jnp.where(lane8 == row8, live, 0.0), axis=1, keepdims=True)
        live_s = jnp.sum(jnp.where(lane8 == row8 + 64, live, 0.0), axis=1, keepdims=True)
        up1[me[1], g * 8 : g * 8 + 8, :] = tile - jnp.where(lane8 < 64, live_c, live_s) * mean
    out_y = spread(1, 3, lambda peer: up1.at[me[1]], lambda s: up1.at[me[1]])
    arrive(halo_f)
    arrive(halo_p)

    @pl.loop(0, 3)
    def _(q):
        message_block(q)

    arrive(out_y)
    all1[me[2]] = jnp.concatenate([up1[c] for c in range(EDGE)], axis=0).astype(BF16)
    out_z = spread(2, 4, lambda peer: all1.at[me[2]], lambda s: all1.at[me[2]])

    @pl.loop(6, 9)
    def _(q):
        message_block(q)

    pre_near = dot(acc[0:ATOMS, :].astype(BF16), wmix_ref[...])
    uv[:, CHANNELS : 2 * CHANNELS] = nbasis[13]

    arrive(out_z)
    prod[0:128, 0:256] = jnp.zeros((128, 256), F32)

    @pl.loop(0, TILES)
    def _(t):
        f_h, f_l = split(filt[t] * all1[t].astype(F32))
        fs_h[t] = f_h
        fs_l[t] = f_l
        prod[0:128, 0:256] += dot3(f_h, f_l, wave_h[t], wave_l[t], TN)

    potential = prod[0:64, 0:128] + prod[64:128, 128:256]
    pre = pre_near + dot(potential.astype(BF16), wlong_ref[...], TN)
    gate = sigmoid(pre)
    refined = own.astype(F32) + pre * gate
    upd_ref[...] = refined.astype(BF16)
    outer = sigmoid(refined)
    readout = rows_ref[1:2, :]
    energy_col = jnp.sum(refined * outer * readout, axis=1, keepdims=True)
    energy_ref[...] = (
        jnp.transpose(jnp.broadcast_to(energy_col, (ATOMS, ATOMS)))[0:1, :] * live_row
    )
    grad_new = live_col * readout * (outer * (1.0 + refined * (1.0 - outer)))
    grad_pre = (grad_new * (gate * (1.0 + pre * (1.0 - gate)))).astype(BF16)
    adjoint = dot(grad_pre, wmix_ref[...], NT).astype(BF16)
    nadj[13] = adjoint
    halo_a = halo(0, 2, nadj)
    wlong2 = jnp.concatenate([wlong_ref[...], wlong_ref[...]], axis=0)
    pull_rows = dot(grad_pre, wlong2, NT)
    p_h, p_l = split(
        jnp.concatenate(
            [jnp.where(half, pull_rows, 0.0), jnp.where(half, 0.0, pull_rows)], axis=0
        )
    )

    @pl.loop(0, TILES)
    def _(t):
        part2[t] = dot3(wave_h[t], wave_l[t], p_h, p_l).astype(BF16)

    red_z = spread(2, 5, lambda peer: part2.at[peer], lambda s: got2z.at[s])

    first = iota((ATOMS, ATOMS), 0) < 64
    pull_t = jnp.transpose(pull_rows)
    neutral_t = jnp.transpose((charge - mean) * live_col)
    pull[0:128, 0:128] = jnp.where(first, 0.0, pull_t)
    pull[0:128, 128:256] = jnp.where(first, pull_t, 0.0)
    pull[128:256, 0:128] = jnp.where(first, 0.0, neutral_t)
    pull[128:256, 128:256] = jnp.where(first, neutral_t, 0.0)

    for b in range(BASES):
        uv[b * ATOMS : b * ATOMS + ATOMS, 0:CHANNELS] = adjoint
    for axis in range(3):
        acc[axis * ATOMS : axis * ATOMS + ATOMS, :] = jnp.zeros((ATOMS, ATOMS), F32)

    def force_block(q):
        for oz in range(3):
            for b in range(BASES):
                rows = slice(b * ATOMS, b * ATOMS + ATOMS)
                near = jnp.concatenate([nbasis[q * 3 + oz, rows, :], nadj[q * 3 + oz]], axis=1)
                prod[rows, oz * 128 : oz * 128 + 128] = dot(uv[rows, :], near, NT)
        for row0 in range(0, ATOMS, STRIP):
            total_x = total_y = total_z = None
            for oz in range(3):
                dx, dy, dz, base, decay = pair(q, oz, row0, STRIP)
                envelope = base * base
                double = base + base
                strength = None
                for b, rate in enumerate((1.0, 3.0, 8.0, 20.0)):
                    got = prod[
                        b * ATOMS + row0 : b * ATOMS + row0 + STRIP, oz * 128 : oz * 128 + 128
                    ]
                    term = decay[b] * (envelope * rate + double) * got
                    strength = term if strength is None else strength + term
                if total_x is None:
                    total_x, total_y, total_z = strength * dx, strength * dy, strength * dz
                else:
                    total_x = total_x + strength * dx
                    total_y = total_y + strength * dy
                    total_z = total_z + strength * dz
            acc[row0 : row0 + STRIP, :] += total_x
            acc[128 + row0 : 128 + row0 + STRIP, :] += total_y
            acc[256 + row0 : 256 + row0 + STRIP, :] += total_z

    arrive(halo_a)
    halo_a = halo(1, 2, nadj)
    force_block(jnp.int32(4))

    arrive(red_z)
    value = reduced(part2[me[2]], got2z)
    for c in range(EDGE):
        mid2[c] = value[c * CHUNK : c * CHUNK + CHUNK, :]
    red_y = spread(1, 6, lambda peer: mid2.at[peer], lambda s: got2y.at[s])
    arrive(halo_a)
    halo_a = halo(2, 2, nadj)
    force_block(jnp.int32(3))
    force_block(jnp.int32(5))

    arrive(red_y)
    low2[...] = reduced(mid2[me[1]], got2y)
    red_x = spread(0, 7, lambda peer: low2, lambda s: got2x.at[s])
    arrive(halo_a)

    @pl.loop(0, 2)
    def _(q):
        force_block(q)

    arrive(red_x)
    up2[me[1]] = reduced(low2[...], got2x)
    out_y = spread(1, 8, lambda peer: up2.at[me[1]], lambda s: up2.at[me[1]])

    @pl.loop(0, 2)
    def _(q):
        force_block(q * 4 + 2)

    arrive(out_y)
    all2[me[2]] = jnp.concatenate([up2[c] for c in range(EDGE)], axis=0).astype(BF16)
    out_z = spread(2, 9, lambda peer: all2.at[me[2]], lambda s: all2.at[me[2]])

    @pl.loop(7, 9)
    def _(q):
        force_block(q)

    lane = iota((ATOMS, ATOMS), 1)
    columns = jnp.zeros((ATOMS, ATOMS), F32)
    for axis in range(3):
        near_sum = jnp.sum(acc[axis * ATOMS : axis * ATOMS + ATOMS, :], axis=1, keepdims=True)
        columns = jnp.where(lane == axis, near_sum, columns)
    near_force = jnp.transpose(columns)[0:8, :] * (-2.0 / CUTOFF2)
    r_h, r_l = split(pull[...])

    arrive(out_z)
    prod[0:8, 0:128] = jnp.zeros((8, 128), F32)

    @pl.loop(0, TILES)
    def _(t):
        b_h, b_l = split(filt[t] * all2[t].astype(F32))
        left_h = jnp.concatenate([fs_h[t], b_h], axis=1)
        left_l = jnp.concatenate([fs_l[t], b_l], axis=1)
        mixed = dot3(left_h, left_l, r_h, r_l)
        waves = wave_f[t]
        d_h, d_l = split(
            waves[:, 0:128] * mixed[:, 0:128] - waves[:, 128:256] * mixed[:, 128:256]
        )
        index = iota((8, ROWS), 1) + t * ROWS
        axis_row = iota((8, ROWS), 0)
        group = lax.shift_right_logical(index, 3)
        group_x = lax.shift_right_logical(group * 79, 10)
        value_x = group_x - TOP
        value_y = group - group_x * SIDE - TOP
        value_z = lax.bitwise_and(index, 7)
        values = jnp.where(axis_row == 0, value_x, jnp.where(axis_row == 1, value_y, value_z))
        rows = values.astype(F32).astype(BF16)
        prod[0:8, 0:128] += dot(rows, d_h) + dot(rows, d_l)

    force = near_force - prod[0:8, 0:128] * (2.0 * math.pi / EDGE)
    force_ref[...] = force[0:3, :]
    for copy in sent:
        copy.wait_send()


def shards(
    features,
    positions,
    counts,
    w_proj,
    w_mix,
    w_long,
    w_charge,
    charge_bias,
    w_energy,
    k_filter,
    k_index,
):
    rows = jnp.stack([jnp.concatenate([charge_bias, charge_bias]), w_energy])
    vmem = pl.BlockSpec(memory_space=pltpu.VMEM)
    dma = pltpu.SemaphoreType.DMA
    reduce_buffers = [
        pltpu.VMEM((TILES, ROWS, 128), BF16),
        pltpu.VMEM((EDGE - 1, ROWS, 128), BF16),
        pltpu.VMEM((EDGE, CHUNK, 128), F32),
        pltpu.VMEM((EDGE - 1, CHUNK, 128), F32),
        pltpu.VMEM((CHUNK, 128), F32),
        pltpu.VMEM((EDGE - 1, CHUNK, 128), F32),
        pltpu.VMEM((EDGE, CHUNK, 128), F32),
        pltpu.VMEM((TILES, ROWS, 128), BF16),
    ]
    updated, energy, force = pl.pallas_call(
        block_kernel,
        name="block",
        out_shape=(
            jax.ShapeDtypeStruct((ATOMS, CHANNELS), BF16),
            jax.ShapeDtypeStruct((1, ATOMS), F32),
            jax.ShapeDtypeStruct((3, ATOMS), F32),
        ),
        in_specs=[pl.BlockSpec(memory_space=pltpu.SMEM)] + [vmem] * 9,
        out_specs=(vmem, vmem, vmem),
        scratch_shapes=[
            pltpu.VMEM((27, ATOMS, CHANNELS), BF16),
            pltpu.VMEM((27, ATOMS, CHANNELS), BF16),
            pltpu.VMEM((27, 8, ATOMS), F32),
            pltpu.VMEM((6, 8, ATOMS), F32),
            pltpu.VMEM((TILES, ROWS, 256), F32),
            pltpu.VMEM((TILES, ROWS, 256), BF16),
            pltpu.VMEM((TILES, ROWS, 256), BF16),
            pltpu.VMEM((TILES, ROWS, 128), F32),
            pltpu.VMEM((TILES, ROWS, 128), BF16),
            pltpu.VMEM((TILES, ROWS, 128), BF16),
        ]
        + reduce_buffers
        + reduce_buffers
        + [
            pltpu.VMEM((8, 128), F32),
            pltpu.VMEM((8, 128), F32),
            pltpu.VMEM((8, 128), F32),
            pltpu.VMEM((3, EDGE - 1, 8, 128), F32),
            pltpu.VMEM((3, ATOMS, ATOMS), F32),
            pltpu.VMEM((ATOMS, 3 * BASES * ATOMS), BF16),
            pltpu.VMEM((CHANNELS, BASES * CHANNELS), BF16),
            pltpu.VMEM((27, BASES * ATOMS, CHANNELS), BF16),
            pltpu.VMEM((BASES * ATOMS, CHANNELS), F32),
            pltpu.VMEM((BASES * ATOMS, 3 * 128), F32),
            pltpu.VMEM((BASES * ATOMS, 2 * CHANNELS), BF16),
            pltpu.VMEM((256, 256), F32),
            dma((10, EDGE - 1)),
            dma((10, EDGE - 1)),
            dma((3, EDGE - 1)),
            dma((3, EDGE - 1)),
            dma((3, 3, 2)),
            dma((3, 3, 2)),
        ],
        compiler_params=pltpu.CompilerParams(
            collective_id=0, has_side_effects=True, vmem_limit_bytes=48 * 1024 * 1024
        ),
    )(
        counts.reshape(1),
        features[0, 0, 0],
        positions[0, 0, 0],
        w_proj,
        w_mix,
        w_long,
        w_charge,
        rows,
        k_filter,
        k_index,
    )
    return (
        updated[None, None, None],
        energy.reshape(1, 1, 1, ATOMS),
        force[None, None, None],
    )


def solution(mesh):
    cells = P("gx", "gy", "gz")
    in_specs = (cells, cells, cells) + (P(),) * 8
    return jax.shard_map(
        shards, mesh=mesh, in_specs=in_specs, out_specs=(cells, cells, cells), check_vma=False
    )
```

```python
import functools
import math

import jax
import jax.numpy as jnp
from jax import lax
from jax.experimental import pallas as pl
from jax.experimental.pallas import tpu as pltpu
from jax.sharding import PartitionSpec as P

MESH = pl.DeviceIdType.MESH
CUTOFF2 = 0.9 * 0.9
ATOMS = 128
CHANNELS = 128
BASES = 4
EDGE = 8
WAVES = 2048
TOP = 6
SIDE = 2 * TOP + 1
TILES = 8
ROWS = 192
PIECES = 1
PIECE = 192
SUB = 24
SLOTS = TILES * ROWS
F32 = jnp.float32
BF16 = jnp.bfloat16
NT = (((1,), (1,)), ((), ()))
NN = (((1,), (0,)), ((), ()))
TN = (((0,), (0,)), ((), ()))


def dot(a, b, dims=NN):
    return lax.dot_general(a, b, dims, preferred_element_type=F32)


def split(value):
    high = value.astype(BF16)
    low = (value - high.astype(F32)).astype(BF16)
    return high, low


def dot3(a_high, a_low, b_high, b_low, dims=NN):
    return dot(a_high, b_high, dims) + dot(a_high, b_low, dims) + dot(a_low, b_high, dims)


def iota(shape, dim):
    return lax.broadcasted_iota(jnp.int32, shape, dim)


def sigmoid(v):
    return 1.0 / (1.0 + jnp.exp(-v))


def block_kernel(
    counts_ref,
    feat_hbm,
    pos_hbm,
    wproj_hbm,
    wmix_hbm,
    wlong_hbm,
    wcharge_hbm,
    bias_hbm,
    wenergy_hbm,
    kf_hbm,
    kidx_hbm,
    upd_ref,
    energy_ref,
    force_ref,
    feat_ref,
    pos_ref,
    wproj_ref,
    wmix_ref,
    wlong_ref,
    wcharge_ref,
    bias_ref,
    wenergy_ref,
    kf_ref,
    kidx_ref,
    nfeat,
    nadj,
    pack,
    trig,
    row,
    wave_f,
    wave_h,
    wave_l,
    filt,
    fs_h,
    fs_l,
    part1,
    gotz1,
    mid1,
    goty1,
    low1,
    gotx1,
    up1,
    full1,
    part2,
    gotz2,
    mid2,
    goty2,
    low2,
    gotx2,
    up2,
    full2,
    pcol,
    rad,
    wcat,
    nbasis,
    acc,
    prod,
    uv,
    pull,
    load_sem,
    send_sem,
    recv_sem,
    hsend,
    hrecv,
):
    me = tuple(lax.axis_index(name) for name in ("gx", "gy", "gz"))

    zcore, yrow, xhalf = lax.rem(me[0], 2), me[1], lax.rem(me[2], 2)
    place = ((me[0] // 2) * 2 + xhalf, yrow, (me[2] // 2) * 2 + zcore)

    def device_at(axis, distance):
        peer = lax.rem(place[axis] + distance, EDGE)
        high, low = (peer // 2) * 2, lax.rem(peer, 2)
        if axis == 0:
            return peer, (high + zcore, me[1], (me[2] // 2) * 2 + low)
        if axis == 1:
            return peer, (me[0], peer, me[2])
        return peer, ((me[0] // 2) * 2 + low, me[1], high + xhalf)

    def cell_at(axis, distance):
        coords = list(me)
        coords[axis] = lax.rem(me[axis] + distance, EDGE)
        return tuple(coords)

    loads = [
        pltpu.make_async_copy(source, target, load_sem.at[i])
        for i, (source, target) in enumerate(
            (
                (pos_hbm, pos_ref),
                (feat_hbm, feat_ref),
                (wcharge_hbm, wcharge_ref),
                (bias_hbm, bias_ref),
                (kidx_hbm, kidx_ref),
                (kf_hbm, kf_ref),
                (wproj_hbm, wproj_ref),
                (wmix_hbm, wmix_ref),
                (wlong_hbm, wlong_ref),
                (wenergy_hbm, wenergy_ref),
            )
        )
    ]
    for load in loads:
        load.start()
    barrier = pltpu.get_barrier_semaphore()
    for axis in range(3):
        for d in range(1, EDGE):
            pl.semaphore_signal(
                barrier, inc=1, device_id=device_at(axis, d)[1], device_id_type=MESH
            )

    for axis in (0, 2):
        for d in (1, EDGE - 1):
            pl.semaphore_signal(
                barrier, inc=1, device_id=cell_at(axis, d), device_id_type=MESH
            )

    sent = []

    def drain():
        for copy in sent:
            copy.wait_send()
        sent.clear()

    def send(src, dst, ssem, rsem, device):
        copy = pltpu.make_async_remote_copy(
            src_ref=src,
            dst_ref=dst,
            send_sem=ssem,
            recv_sem=rsem,
            device_id=device,
            device_id_type=MESH,
        )
        copy.start()
        sent.append(copy)
        return copy

    def spread(axis, slot, source, target):
        copies = []
        for d in range(1, EDGE):
            peer, device = device_at(axis, d)
            copies.append(
                send(
                    source(peer),
                    target(d - 1),
                    send_sem.at[slot + (d - 1,)],
                    recv_sem.at[slot + (d - 1,)],
                    device,
                )
            )
        return copies

    def arrive(copies):
        for copy in copies:
            copy.wait_recv()

    def tile_at(distance):
        return lax.rem(place[2] + distance, EDGE)

    def send_tile(kind, part, gotz, d):
        peer, device = device_at(2, d)
        copies = []
        for p in range(PIECES):
            rows = pl.ds(p * PIECE, PIECE)
            copies.append(
                send(
                    part.at[peer, rows],
                    gotz.at[d - 1, rows],
                    send_sem.at[kind, 0, p, d - 1],
                    recv_sem.at[kind, 0, p, d - 1],
                    device,
                )
            )
        return copies

    def reduce_gather(kind, tiles, part, gotz, mid, goty, low, gotx, up, full, finish, hook):
        stages = []
        for p in range(PIECES):
            arrive([copies[p] for copies in tiles])
            rows = slice(p * PIECE, p * PIECE + PIECE)
            value = part[place[2], rows, :].astype(F32)
            for d in range(1, EDGE):
                value = value + gotz[d - 1, rows, :].astype(F32)
            for c in range(EDGE):
                mid[p, c] = value[c * SUB : c * SUB + SUB, :]
            stages.append(
                spread(
                    1, (kind, 1, p), lambda peer: mid.at[p, peer], lambda s: goty.at[s, p]
                )
            )
        hook(0)
        copies, stages = stages, []
        for p in range(PIECES):
            arrive(copies[p])
            value = mid[p, place[1]]
            for d in range(1, EDGE):
                value = value + goty[d - 1, p]
            low[p] = value
            stages.append(
                spread(0, (kind, 2, p), lambda peer: low.at[p], lambda s: gotx.at[s, p])
            )
        hook(1)
        copies, stages = stages, []
        for p in range(PIECES):
            arrive(copies[p])
            value = low[p]
            for d in range(1, EDGE):
                value = value + gotx[d - 1, p]
            up[p, place[1]] = finish(value).astype(BF16)
            stages.append(
                spread(
                    1, (kind, 3, p), lambda peer: up.at[p, place[1]], lambda s: up.at[p, place[1]]
                )
            )
        hook(2)
        copies, stages = stages, []
        for p in range(PIECES):
            arrive(copies[p])
            rows = pl.ds(p * PIECE, PIECE)
            full[place[2], p * PIECE : p * PIECE + PIECE, :] = jnp.concatenate(
                [up[p, c].astype(F32) for c in range(EDGE)], axis=0
            ).astype(BF16)
            stages.append(
                spread(
                    2,
                    (kind, 4, p),
                    lambda peer: full.at[place[2], rows],
                    lambda s: full.at[place[2], rows],
                )
            )
        hook(3)
        return stages

    live_row = (iota((1, ATOMS), 1) < counts_ref[0]).astype(F32)
    live_col = (iota((ATOMS, CHANNELS), 0) < counts_ref[0]).astype(F32)
    row[...] = jnp.zeros((8, 128), F32)
    pack[...] = jnp.zeros((16, 128), F32)
    loads[0].wait()

    steps = iota((8, ATOMS), 0).astype(F32)
    for axis in range(3):
        unit = (pos_ref[axis] + me[axis].astype(F32)) * (1.0 / EDGE)
        orders = steps if axis < 2 else jnp.where(steps > 6.5, 0.0, steps)
        turns = orders * unit
        angle = (turns - jnp.floor(turns + 0.5)) * (2.0 * math.pi)
        trig[2 * axis] = jnp.cos(angle)
        trig[2 * axis + 1] = jnp.sin(angle)
    loads[1].wait()
    loads[2].wait()
    loads[3].wait()
    own = feat_ref[...]
    masked = own * live_col.astype(BF16)
    nfeat[13, 0:ATOMS, :] = masked
    for axis in range(3):
        rest = pos_ref[axis]
        for step in range(3):
            digit = rest.astype(BF16).astype(F32)
            pack[3 * step + axis : 3 * step + axis + 1, :] = digit
            rest = rest - digit
    nfeat[13, ATOMS : ATOMS + 16, :] = pack[...].astype(BF16)

    wcharge2 = jnp.concatenate([wcharge_ref[...], wcharge_ref[...]], axis=0)
    row[0:1, 0:64] = bias_ref[...]
    bias = row[...]
    charge_pre = dot(masked, wcharge2, NT) + (bias + pltpu.roll(bias, 64, axis=1))[0:1, :]
    charge = charge_pre * sigmoid(charge_pre) * live_col
    own_total = jnp.broadcast_to(jnp.sum(charge, axis=0, keepdims=True), (8, 128))
    own_count = jnp.broadcast_to(jnp.sum(live_col, axis=0, keepdims=True), (8, 128))
    z_c = trig[4]
    z_s = trig[5]
    y_c = [jnp.broadcast_to(trig[2, m : m + 1, :], (8, ATOMS)) for m in range(TOP + 1)]
    y_s = [jnp.broadcast_to(trig[3, m : m + 1, :], (8, ATOMS)) for m in range(TOP + 1)]

    def put_wave(group, c, s):
        tile, row = group // 24, (group % 24) * 8
        wave_f[tile, row : row + 8, 0:ATOMS] = c
        wave_f[tile, row : row + 8, ATOMS : 2 * ATOMS] = s

    for kx in range(-TOP, TOP + 1):
        x_c = trig[0, abs(kx) : abs(kx) + 1, :]
        x_s = trig[1, abs(kx) : abs(kx) + 1, :]
        if kx < 0:
            x_s = -x_s
        xz_c = x_c * z_c - x_s * z_s
        xz_s = x_c * z_s + x_s * z_c
        base = (kx + TOP) * SIDE + TOP
        put_wave(base, xz_c, xz_s)
        for ky in range(1, TOP + 1):
            cc, ss = xz_c * y_c[ky], xz_s * y_s[ky]
            cs, sc = xz_c * y_s[ky], xz_s * y_c[ky]
            put_wave(base + ky, cc - ss, cs + sc)
            put_wave(base - ky, cc + ss, sc - cs)
    for group in range(SIDE * SIDE, SLOTS // 8):
        put_wave(group, jnp.zeros((8, ATOMS), F32), jnp.zeros((8, ATOMS), F32))

    half = iota((ATOMS, ATOMS), 1) < 64
    q_h, q_l = split(
        jnp.concatenate([jnp.where(half, charge, 0.0), jnp.where(half, 0.0, charge)], axis=0)
    )
    acc[0:128, :] = jnp.zeros((128, 128), F32)
    acc[128:256, :] = jnp.zeros((128, 128), F32)
    acc[0:8, :] = z_c * live_row
    acc[64:72, :] = z_s * live_row
    acc[128:136, :] = -(z_s * live_row)
    acc[192:200, :] = z_c * live_row
    live_rhs = jnp.concatenate(
        [jnp.transpose(acc[0:128, :]), jnp.transpose(acc[128:256, :])], axis=0
    )
    l_h, l_l = split(live_rhs)
    both_h = jnp.concatenate([q_h, l_h], axis=1)
    both_l = jnp.concatenate([q_l, l_l], axis=1)
    spare = lax.rem(iota((ROWS, 128), 0), 8) == 7

    pl.semaphore_wait(barrier, 3 * (EDGE - 1) + 4)

    def shift(axis, stage, kind, buffer, source, before, after, width):
        ring = []
        for side, distance in ((0, 1), (1, EDGE - 1)):
            start = before if side == 0 else after
            tag = (kind, stage, side)
            ring.append(
                send(
                    buffer.at[pl.ds(source, width)] if width > 1 else buffer.at[source],
                    buffer.at[pl.ds(start, width)] if width > 1 else buffer.at[start],
                    hsend.at[tag],
                    hrecv.at[tag],
                    cell_at(axis, distance),
                )
            )
        return ring

    def halo(stage, kind, buffer):
        if stage == 0:
            return shift(2, 0, kind, buffer, 13, 12, 14, 1)
        if stage == 1:
            return shift(0, 1, kind, buffer, 12, 9, 15, 3)
        column = (1, 0, 2)[stage - 2] * 3
        return shift(1, stage, kind, buffer, 9 + column, column, 18 + column, 3)

    halo_f = halo(0, 0, nfeat)
    lane8 = iota((8, 128), 1)
    row8 = iota((8, 128), 0)
    moved = jnp.where(lane8 == 16, own_count, pltpu.roll(own_total, 8, axis=1))
    lanes = iota((ROWS, 128), 1)
    member = lax.rem(iota((ROWS, 128), 0), 24) // 8
    first_free = (member == 0) & (lanes >= 8) & (lanes < 64)
    second_free = (member == 1) & (lanes >= 8) & (lanes <= 16)
    extra = jnp.where(first_free, own_total[0:1, :], jnp.where(second_free, moved[0:1, :], 0.0))
    tiles = []
    for d in (4, 3, 5, 2, 6, 1, 7, 0):
        t = tile_at(d)
        w_h, w_l = split(wave_f[t])
        wave_h[t] = w_h
        wave_l[t] = w_l
        sums = dot3(w_h, w_l, both_h, both_l)
        part1[t] = jnp.where(spare, sums[:, 128:256] + extra, sums[:, 0:128]).astype(BF16)
        if d > 0:
            tiles.append(send_tile(0, part1, gotz1, d))

    for load in loads[4:]:
        load.wait()
    k_h, k_l = split(kf_ref[...])
    kf2 = jnp.concatenate([k_h, k_l], axis=0)
    kx, ky, kz = kidx_ref[0:1, :], kidx_ref[1:2, :], kidx_ref[2:3, :]
    sign = jnp.where(kz < 0, -1, 1)
    slot = ((kx * sign + TOP) * SIDE + (ky * sign + TOP)) * 8 + kz * sign
    scale = 4.0 / math.sqrt(ATOMS * EDGE * EDGE * EDGE * WAVES)

    @pl.loop(0, TILES)
    def _(t):
        hot = jnp.where(iota((ROWS, WAVES), 0) + t * ROWS == slot, 1.0, 0.0).astype(BF16)
        part = dot(hot, kf2, NT)
        filt[t] = (part + pltpu.roll(part, 64, axis=1)) * scale

    for axis in range(3):
        pcol[axis] = jnp.transpose(jnp.broadcast_to(pos_ref[axis], (ATOMS, ATOMS)))
    acc[0:ATOMS, :] = jnp.zeros((ATOMS, CHANNELS), F32)
    for b in range(BASES):
        wcat[:, b * CHANNELS : b * CHANNELS + CHANNELS] = wproj_ref[b]

    def pair(q, oz, row0, rows):
        digits = nfeat[q * 3 + oz, ATOMS : ATOMS + 16, :].astype(F32)
        where = digits[0:3, :] + (digits[3:6, :] + digits[6:9, :])
        shift_y = (q // 3 - 1).astype(F32)
        shift_x = (lax.rem(q, 3) - 1).astype(F32)
        dx = (where[0:1, :] + shift_x) - pcol[0, row0 : row0 + rows, :]
        dy = (where[1:2, :] + shift_y) - pcol[1, row0 : row0 + rows, :]
        dz = (where[2:3, :] + float(oz - 1)) - pcol[2, row0 : row0 + rows, :]
        scaled = (dx * dx + dy * dy + dz * dz) * (1.0 / CUTOFF2)
        base = jnp.maximum(1.0 - scaled, 0.0)
        if oz == 1:
            same = iota((rows, ATOMS), 0) + row0 == iota((rows, ATOMS), 1)
            base = base * jnp.where(same, jnp.where(q == 4, 0.0, 1.0), 1.0)
        e1 = jnp.exp(-scaled)
        e2 = e1 * e1
        e3 = e2 * e1
        e4 = e2 * e2
        e8 = e4 * e4
        e20 = e8 * e8 * e4
        return dx, dy, dz, base, (e1, e3, e8, e20)

    STRIP = 32

    def message_block(q):
        for oz in range(3):
            for row0 in range(0, ATOMS, STRIP):
                _, _, _, base, decay = pair(q, oz, row0, STRIP)
                envelope = base * base
                for b in range(BASES):
                    column = (oz * BASES + b) * ATOMS
                    rad[row0 : row0 + STRIP, column : column + ATOMS] = (
                        decay[b] * envelope
                    ).astype(BF16)
            values = dot(nfeat[q * 3 + oz, 0:ATOMS, :], wcat[...]).astype(BF16)
            for b in range(BASES):
                nbasis[q * 3 + oz, b * ATOMS : b * ATOMS + ATOMS, :] = values[
                    :, b * CHANNELS : b * CHANNELS + CHANNELS
                ]
        near = nbasis[pl.ds(q * 3, 3)].reshape(3 * BASES * ATOMS, CHANNELS)
        acc[0:ATOMS, :] += dot(rad[...], near)

    state = {"halo": halo_f}

    def hook1(step):
        if step == 0:
            arrive(state["halo"])
            state["halo"] = halo(1, 0, nfeat)
            message_block(jnp.int32(4))
        elif step == 1:
            arrive(state["halo"])
            state["halo"] = halo(2, 0, nfeat)
            state["more"] = halo(3, 0, nfeat)
            message_block(jnp.int32(3))
            message_block(jnp.int32(5))
        elif step == 2:
            arrive(state["halo"])
            message_block(jnp.int32(1))
            message_block(jnp.int32(7))
        else:
            last = halo(4, 0, nfeat)
            arrive(state["more"])
            message_block(jnp.int32(0))
            message_block(jnp.int32(6))
            arrive(last)
            message_block(jnp.int32(2))
            message_block(jnp.int32(8))

    def neutralise(value):
        row0 = jnp.broadcast_to(value[7:8, :], (8, 128))
        row1 = jnp.broadcast_to(value[15:16, :], (8, 128))
        total = jnp.where(lane8 < 8, pltpu.roll(row1, 120, axis=1), row0)
        total = jnp.where(lane8 < 64, total, pltpu.roll(total, 64, axis=1))
        count = jnp.sum(jnp.where(lane8 == 16, row1, 0.0), axis=1, keepdims=True)
        state["mean"] = (total / count)[0:1, :]
        parts = []
        for g in range(0, SUB, 8):
            tile = value[g : g + 8, :]
            live = jnp.broadcast_to(tile[7:8, :], (8, 128))
            live_c = jnp.sum(jnp.where(lane8 == row8, live, 0.0), axis=1, keepdims=True)
            live_s = jnp.sum(jnp.where(lane8 == row8 + 64, live, 0.0), axis=1, keepdims=True)
            parts.append(tile - jnp.where(lane8 < 64, live_c, live_s) * state["mean"])
        return jnp.concatenate(parts, axis=0)

    out_z = reduce_gather(
        0, tiles, part1, gotz1, mid1, goty1, low1, gotx1, up1, full1, neutralise, hook1
    )
    mean = state["mean"]

    pre_near = dot(acc[0:ATOMS, :].astype(BF16), wmix_ref[...])
    uv[:, CHANNELS : 2 * CHANNELS] = nbasis[13]

    prod[0:128, 0:256] = jnp.zeros((128, 256), F32)
    for d in range(EDGE):
        if d > 0:
            arrive([copies[d - 1] for copies in out_z])
        t = tile_at(EDGE - d)
        f_h, f_l = split(filt[t] * full1[t].astype(F32))
        fs_h[t] = f_h
        fs_l[t] = f_l
        prod[0:128, 0:256] += dot3(f_h, f_l, wave_h[t], wave_l[t], TN)

    potential = prod[0:64, 0:128] + prod[64:128, 128:256]
    pre = pre_near + dot(potential.astype(BF16), wlong_ref[...], TN)
    gate = sigmoid(pre)
    refined = own.astype(F32) + pre * gate
    outer = sigmoid(refined)
    readout = wenergy_ref[...]
    grad_new = live_col * readout * (outer * (1.0 + refined * (1.0 - outer)))
    grad_pre = (grad_new * (gate * (1.0 + pre * (1.0 - gate)))).astype(BF16)
    adjoint = dot(grad_pre, wmix_ref[...], NT).astype(BF16)
    nadj[13] = adjoint
    wlong2 = jnp.concatenate([wlong_ref[...], wlong_ref[...]], axis=0)
    pull_rows = dot(grad_pre, wlong2, NT)
    p_h, p_l = split(
        jnp.concatenate(
            [jnp.where(half, pull_rows, 0.0), jnp.where(half, 0.0, pull_rows)], axis=0
        )
    )

    tiles = []
    for d in (4, 3, 5, 2, 6, 1, 7, 0):
        t = tile_at(d)
        part2[t] = dot3(wave_h[t], wave_l[t], p_h, p_l).astype(BF16)
        if d > 0:
            tiles.append(send_tile(1, part2, gotz2, d))
    state["halo"] = halo(0, 1, nadj)

    upd_ref[...] = refined.astype(BF16)
    energy_col = jnp.sum(refined * outer * readout, axis=1, keepdims=True)
    energy_ref[...] = (
        jnp.transpose(jnp.broadcast_to(energy_col, (ATOMS, ATOMS)))[0:1, :] * live_row
    )

    first = iota((ATOMS, ATOMS), 0) < 64
    pull_t = jnp.transpose(pull_rows)
    neutral_t = jnp.transpose((charge - mean) * live_col)
    pull[0:128, 0:128] = jnp.where(first, 0.0, pull_t)
    pull[0:128, 128:256] = jnp.where(first, pull_t, 0.0)
    pull[128:256, 0:128] = jnp.where(first, 0.0, neutral_t)
    pull[128:256, 128:256] = jnp.where(first, neutral_t, 0.0)

    for b in range(BASES):
        uv[b * ATOMS : b * ATOMS + ATOMS, 0:CHANNELS] = adjoint
    for axis in range(3):
        acc[axis * ATOMS : axis * ATOMS + ATOMS, :] = jnp.zeros((ATOMS, ATOMS), F32)

    def force_block(q):
        for oz in range(3):
            for b in range(BASES):
                rows = slice(b * ATOMS, b * ATOMS + ATOMS)
                near = jnp.concatenate([nbasis[q * 3 + oz, rows, :], nadj[q * 3 + oz]], axis=1)
                prod[rows, oz * 128 : oz * 128 + 128] = dot(uv[rows, :], near, NT)
        for row0 in range(0, ATOMS, STRIP):
            total_x = total_y = total_z = None
            for oz in range(3):
                dx, dy, dz, base, decay = pair(q, oz, row0, STRIP)
                envelope = base * base
                double = base + base
                strength = None
                for b, rate in enumerate((1.0, 3.0, 8.0, 20.0)):
                    got = prod[
                        b * ATOMS + row0 : b * ATOMS + row0 + STRIP, oz * 128 : oz * 128 + 128
                    ]
                    term = decay[b] * (envelope * rate + double) * got
                    strength = term if strength is None else strength + term
                if total_x is None:
                    total_x, total_y, total_z = strength * dx, strength * dy, strength * dz
                else:
                    total_x = total_x + strength * dx
                    total_y = total_y + strength * dy
                    total_z = total_z + strength * dz
            acc[row0 : row0 + STRIP, :] += total_x
            acc[128 + row0 : 128 + row0 + STRIP, :] += total_y
            acc[256 + row0 : 256 + row0 + STRIP, :] += total_z

    def hook2(step):
        if step != 3:
            drain()
        if step == 0:
            arrive(state["halo"])
            state["halo"] = halo(1, 1, nadj)
            force_block(jnp.int32(4))
        elif step == 1:
            arrive(state["halo"])
            state["halo"] = halo(2, 1, nadj)
            state["more"] = halo(3, 1, nadj)
            force_block(jnp.int32(3))
            force_block(jnp.int32(5))
        elif step == 2:
            arrive(state["halo"])
            force_block(jnp.int32(1))
            force_block(jnp.int32(7))
        else:
            last = halo(4, 1, nadj)
            arrive(state["more"])
            force_block(jnp.int32(0))
            force_block(jnp.int32(6))
            arrive(last)
            force_block(jnp.int32(2))
            force_block(jnp.int32(8))

    out_z = reduce_gather(
        1, tiles, part2, gotz2, mid2, goty2, low2, gotx2, up2, full2, lambda v: v, hook2
    )

    lane = iota((ATOMS, ATOMS), 1)
    columns = jnp.zeros((ATOMS, ATOMS), F32)
    for axis in range(3):
        near_sum = jnp.sum(acc[axis * ATOMS : axis * ATOMS + ATOMS, :], axis=1, keepdims=True)
        columns = jnp.where(lane == axis, near_sum, columns)
    near_force = jnp.transpose(columns)[0:8, :] * (-2.0 / CUTOFF2)
    r_h, r_l = split(pull[...])

    prod[0:8, 0:128] = jnp.zeros((8, 128), F32)
    for d in range(EDGE):
        if d > 0:
            arrive([copies[d - 1] for copies in out_z])
        t = tile_at(EDGE - d)
        b_h, b_l = split(filt[t] * full2[t].astype(F32))
        left_h = jnp.concatenate([fs_h[t], b_h], axis=1)
        left_l = jnp.concatenate([fs_l[t], b_l], axis=1)
        mixed = dot3(left_h, left_l, r_h, r_l)
        waves = wave_f[t]
        d_h, d_l = split(
            waves[:, 0:128] * mixed[:, 0:128] - waves[:, 128:256] * mixed[:, 128:256]
        )
        index = iota((8, ROWS), 1) + t * ROWS
        axis_row = iota((8, ROWS), 0)
        group = lax.shift_right_logical(index, 3)
        group_x = lax.shift_right_logical(group * 79, 10)
        value_x = group_x - TOP
        value_y = group - group_x * SIDE - TOP
        value_z = lax.bitwise_and(index, 7)
        values = jnp.where(axis_row == 0, value_x, jnp.where(axis_row == 1, value_y, value_z))
        rows = values.astype(F32).astype(BF16)
        prod[0:8, 0:128] += dot(rows, d_h) + dot(rows, d_l)

    force = near_force - prod[0:8, 0:128] * (2.0 * math.pi / EDGE)
    for axis in range(3):
        force_ref[axis] = force[axis : axis + 1, :]
    drain()


def shards(
    features,
    positions,
    counts,
    w_proj,
    w_mix,
    w_long,
    w_charge,
    charge_bias,
    w_energy,
    k_filter,
    k_index,
):
    hbm = pl.BlockSpec(memory_space=pltpu.HBM)
    vmem = pl.BlockSpec(memory_space=pltpu.VMEM)
    dma = pltpu.SemaphoreType.DMA
    reduce_buffers = [
        pltpu.VMEM((TILES, ROWS, 128), BF16),
        pltpu.VMEM((EDGE - 1, ROWS, 128), BF16),
        pltpu.VMEM((PIECES, EDGE, SUB, 128), F32),
        pltpu.VMEM((EDGE - 1, PIECES, SUB, 128), F32),
        pltpu.VMEM((PIECES, SUB, 128), F32),
        pltpu.VMEM((EDGE - 1, PIECES, SUB, 128), F32),
        pltpu.VMEM((PIECES, EDGE, SUB, 128), BF16),
        pltpu.VMEM((TILES, ROWS, 128), BF16),
    ]
    updated, energy, force = pl.pallas_call(
        block_kernel,
        name="block",
        out_shape=(
            jax.ShapeDtypeStruct((ATOMS, CHANNELS), BF16),
            jax.ShapeDtypeStruct((1, ATOMS), F32),
            jax.ShapeDtypeStruct((3, 1, ATOMS), F32),
        ),
        in_specs=[pl.BlockSpec(memory_space=pltpu.SMEM)] + [hbm] * 10,
        out_specs=(vmem, vmem, vmem),
        scratch_shapes=[
            pltpu.VMEM((ATOMS, CHANNELS), BF16),
            pltpu.VMEM((3, 1, ATOMS), F32),
            pltpu.VMEM((BASES, CHANNELS, CHANNELS), BF16),
            pltpu.VMEM((CHANNELS, CHANNELS), BF16),
            pltpu.VMEM((64, CHANNELS), BF16),
            pltpu.VMEM((64, CHANNELS), BF16),
            pltpu.VMEM((1, 64), F32),
            pltpu.VMEM((1, CHANNELS), F32),
            pltpu.VMEM((64, WAVES), F32),
            pltpu.VMEM((3, WAVES), jnp.int32),
            pltpu.VMEM((27, ATOMS + 16, CHANNELS), BF16),
            pltpu.VMEM((27, ATOMS, CHANNELS), BF16),
            pltpu.VMEM((16, ATOMS), F32),
            pltpu.VMEM((6, 8, ATOMS), F32),
            pltpu.VMEM((8, 128), F32),
            pltpu.VMEM((TILES, ROWS, 256), F32),
            pltpu.VMEM((TILES, ROWS, 256), BF16),
            pltpu.VMEM((TILES, ROWS, 256), BF16),
            pltpu.VMEM((TILES, ROWS, 128), F32),
            pltpu.VMEM((TILES, ROWS, 128), BF16),
            pltpu.VMEM((TILES, ROWS, 128), BF16),
        ]
        + reduce_buffers
        + reduce_buffers
        + [
            pltpu.VMEM((3, ATOMS, ATOMS), F32),
            pltpu.VMEM((ATOMS, 3 * BASES * ATOMS), BF16),
            pltpu.VMEM((CHANNELS, BASES * CHANNELS), BF16),
            pltpu.VMEM((27, BASES * ATOMS, CHANNELS), BF16),
            pltpu.VMEM((BASES * ATOMS, CHANNELS), F32),
            pltpu.VMEM((BASES * ATOMS, 3 * 128), F32),
            pltpu.VMEM((BASES * ATOMS, 2 * CHANNELS), BF16),
            pltpu.VMEM((256, 256), F32),
            dma((10,)),
            dma((2, 5, PIECES, EDGE - 1)),
            dma((2, 5, PIECES, EDGE - 1)),
            dma((2, 5, 2)),
            dma((2, 5, 2)),
        ],
        compiler_params=pltpu.CompilerParams(
            collective_id=0, has_side_effects=True, vmem_limit_bytes=67043328
        ),
    )(
        counts.reshape(1),
        features[0, 0, 0],
        positions.reshape(3, 1, ATOMS),
        w_proj,
        w_mix,
        w_long,
        w_charge,
        charge_bias.reshape(1, 64),
        w_energy.reshape(1, CHANNELS),
        k_filter,
        k_index,
    )
    return (
        updated[None, None, None],
        energy.reshape(1, 1, 1, ATOMS),
        force.reshape(1, 1, 1, 3, ATOMS),
    )


def solution(mesh):
    cells = P("gx", "gy", "gz")
    in_specs = (cells, cells, cells) + (P(),) * 8
    return jax.shard_map(
        shards, mesh=mesh, in_specs=in_specs, out_specs=(cells, cells, cells), check_vma=False
    )
```

```python
import functools
import math

import jax
import jax.numpy as jnp
from jax import lax
from jax.experimental import pallas as pl
from jax.experimental.pallas import tpu as pltpu
from jax.sharding import PartitionSpec as P

MESH = pl.DeviceIdType.MESH
CUTOFF2 = 0.9 * 0.9
ATOMS = 128
CHANNELS = 128
BASES = 4
EDGE = 8
WAVES = 2048
TOP = 6
SIDE = 2 * TOP + 1
TILES = 8
ROWS = 176
GROUPS = 22
PIECES = 1
PIECE = 176
SUB = 24
SLOTS = TILES * ROWS
F32 = jnp.float32
BF16 = jnp.bfloat16
NT = (((1,), (1,)), ((), ()))
NN = (((1,), (0,)), ((), ()))
TN = (((0,), (0,)), ((), ()))


def dot(a, b, dims=NN):
    return lax.dot_general(a, b, dims, preferred_element_type=F32)


def split(value):
    high = value.astype(BF16)
    low = (value - high.astype(F32)).astype(BF16)
    return high, low


def dot3(a_high, a_low, b_high, b_low, dims=NN):
    return dot(a_high, b_high, dims) + dot(a_high, b_low, dims) + dot(a_low, b_high, dims)


def iota(shape, dim):
    return lax.broadcasted_iota(jnp.int32, shape, dim)


def sigmoid(v):
    return 1.0 / (1.0 + jnp.exp(-v))


def block_kernel(
    counts_ref,
    feat_hbm,
    pos_hbm,
    wproj_hbm,
    wmix_hbm,
    wlong_hbm,
    wcharge_hbm,
    bias_hbm,
    wenergy_hbm,
    kf_hbm,
    kidx_hbm,
    upd_ref,
    energy_ref,
    force_ref,
    feat_ref,
    pos_ref,
    wproj_ref,
    wmix_ref,
    wlong_ref,
    wcharge_ref,
    bias_ref,
    wenergy_ref,
    kf_ref,
    kidx_ref,
    nfeat,
    nadj,
    pack,
    trig,
    row,
    wave_f,
    wave_h,
    wave_l,
    filt,
    fs_h,
    fs_l,
    part1,
    gotz1,
    mid1,
    goty1,
    low1,
    gotx1,
    up1,
    full1,
    part2,
    gotz2,
    mid2,
    goty2,
    low2,
    gotx2,
    up2,
    full2,
    pcol,
    rad,
    wcat,
    nbasis,
    acc,
    prod,
    uv,
    pull,
    load_sem,
    send_sem,
    recv_sem,
    hsend,
    hrecv,
):
    me = tuple(lax.axis_index(name) for name in ("gx", "gy", "gz"))

    zcore, yrow, xhalf = lax.rem(me[0], 2), me[1], lax.rem(me[2], 2)
    place = ((me[0] // 2) * 2 + xhalf, yrow, (me[2] // 2) * 2 + zcore)

    def device_at(axis, distance):
        peer = lax.rem(place[axis] + distance, EDGE)
        high, low = (peer // 2) * 2, lax.rem(peer, 2)
        if axis == 0:
            return peer, (high + zcore, me[1], (me[2] // 2) * 2 + low)
        if axis == 1:
            return peer, (me[0], peer, me[2])
        return peer, ((me[0] // 2) * 2 + low, me[1], high + xhalf)

    def cell_at(axis, distance):
        coords = list(me)
        coords[axis] = lax.rem(me[axis] + distance, EDGE)
        return tuple(coords)

    loads = [
        pltpu.make_async_copy(source, target, load_sem.at[i])
        for i, (source, target) in enumerate(
            (
                (pos_hbm, pos_ref),
                (feat_hbm, feat_ref),
                (wcharge_hbm, wcharge_ref),
                (bias_hbm, bias_ref),
                (kidx_hbm, kidx_ref),
                (kf_hbm, kf_ref),
                (wproj_hbm, wproj_ref),
                (wmix_hbm, wmix_ref),
                (wlong_hbm, wlong_ref),
                (wenergy_hbm, wenergy_ref),
            )
        )
    ]
    for load in loads:
        load.start()
    barrier = pltpu.get_barrier_semaphore()
    for axis in range(3):
        for d in range(1, EDGE):
            pl.semaphore_signal(
                barrier, inc=1, device_id=device_at(axis, d)[1], device_id_type=MESH
            )

    for axis in (0, 2):
        for d in (1, EDGE - 1):
            pl.semaphore_signal(
                barrier, inc=1, device_id=cell_at(axis, d), device_id_type=MESH
            )

    sent = []

    def drain():
        for copy in sent:
            copy.wait_send()
        sent.clear()

    def send(src, dst, ssem, rsem, device):
        copy = pltpu.make_async_remote_copy(
            src_ref=src,
            dst_ref=dst,
            send_sem=ssem,
            recv_sem=rsem,
            device_id=device,
            device_id_type=MESH,
        )
        copy.start()
        sent.append(copy)
        return copy

    def spread(axis, slot, source, target):
        copies = []
        for d in range(1, EDGE):
            peer, device = device_at(axis, d)
            copies.append(
                send(
                    source(peer),
                    target(d - 1),
                    send_sem.at[slot + (d - 1,)],
                    recv_sem.at[slot + (d - 1,)],
                    device,
                )
            )
        return copies

    def arrive(copies):
        for copy in copies:
            copy.wait_recv()

    def tile_at(distance):
        return lax.rem(place[2] + distance, EDGE)

    def send_tile(kind, part, gotz, d):
        peer, device = device_at(2, d)
        copies = []
        for p in range(PIECES):
            rows = pl.ds(p * PIECE, PIECE)
            copies.append(
                send(
                    part.at[peer, rows],
                    gotz.at[d - 1, rows],
                    send_sem.at[kind, 0, p, d - 1],
                    recv_sem.at[kind, 0, p, d - 1],
                    device,
                )
            )
        return copies

    def reduce_gather(kind, tiles, part, gotz, mid, goty, low, gotx, up, full, finish, hook):
        stages = []
        for p in range(PIECES):
            arrive([copies[p] for copies in tiles])
            rows = slice(p * PIECE, p * PIECE + PIECE)
            value = part[place[2], rows, :].astype(F32)
            for d in range(1, EDGE):
                value = value + gotz[d - 1, rows, :].astype(F32)
            for c in range(EDGE):
                rows = value[c * SUB : min(c * SUB + SUB, PIECE), :]
                short = SUB - rows.shape[0]
                if short:
                    rows = jnp.concatenate([rows, jnp.zeros((short, 128), F32)], axis=0)
                mid[p, c] = rows.astype(mid.dtype)
            stages.append(
                spread(
                    1, (kind, 1, p), lambda peer: mid.at[p, peer], lambda s: goty.at[s, p]
                )
            )
        hook(0)
        copies, stages = stages, []
        for p in range(PIECES):
            arrive(copies[p])
            value = mid[p, place[1]].astype(F32)
            for d in range(1, EDGE):
                value = value + goty[d - 1, p].astype(F32)
            low[p] = value.astype(low.dtype)
            stages.append(
                spread(0, (kind, 2, p), lambda peer: low.at[p], lambda s: gotx.at[s, p])
            )
        hook(1)
        copies, stages = stages, []
        for p in range(PIECES):
            arrive(copies[p])
            value = low[p].astype(F32)
            for d in range(1, EDGE):
                value = value + gotx[d - 1, p].astype(F32)
            up[p, place[1]] = finish(value).astype(BF16)
            stages.append(
                spread(
                    1, (kind, 3, p), lambda peer: up.at[p, place[1]], lambda s: up.at[p, place[1]]
                )
            )
        hook(2)
        copies, stages = stages, []
        for p in range(PIECES):
            arrive(copies[p])
            rows = pl.ds(p * PIECE, PIECE)
            full[place[2], p * PIECE : p * PIECE + PIECE, :] = jnp.concatenate(
                [
                    up[p, c, 0 : min(SUB, PIECE - c * SUB), :].astype(F32)
                    for c in range(EDGE)
                ],
                axis=0,
            ).astype(BF16)
            stages.append(
                spread(
                    2,
                    (kind, 4, p),
                    lambda peer: full.at[place[2], rows],
                    lambda s: full.at[place[2], rows],
                )
            )
        hook(3)
        return stages

    live_row = (iota((1, ATOMS), 1) < counts_ref[0]).astype(F32)
    live_col = (iota((ATOMS, CHANNELS), 0) < counts_ref[0]).astype(F32)
    row[...] = jnp.zeros((8, 128), F32)
    pack[...] = jnp.zeros((16, 128), F32)
    loads[0].wait()

    steps = iota((8, ATOMS), 0).astype(F32)
    for axis in range(3):
        unit = (pos_ref[axis] + me[axis].astype(F32)) * (1.0 / EDGE)
        orders = steps if axis < 2 else jnp.where(steps > 6.5, 0.0, steps)
        turns = orders * unit
        angle = (turns - jnp.floor(turns + 0.5)) * (2.0 * math.pi)
        trig[2 * axis] = jnp.cos(angle)
        trig[2 * axis + 1] = jnp.sin(angle)
    loads[1].wait()
    loads[2].wait()
    loads[3].wait()
    own = feat_ref[...]
    masked = own * live_col.astype(BF16)
    nfeat[13, 0:ATOMS, :] = masked
    for axis in range(3):
        rest = pos_ref[axis]
        for step in range(3):
            digit = rest.astype(BF16).astype(F32)
            pack[3 * step + axis : 3 * step + axis + 1, :] = digit
            rest = rest - digit
    nfeat[13, ATOMS : ATOMS + 16, :] = pack[...].astype(BF16)

    wcharge2 = jnp.concatenate([wcharge_ref[...], wcharge_ref[...]], axis=0)
    row[0:1, 0:64] = bias_ref[...]
    bias = row[...]
    bias_row = (bias + pltpu.roll(bias, 64, axis=1))[0:1, :]
    charge_pre = dot(masked, wcharge2, NT) + bias_row
    squares = wcharge2.astype(F32) * wcharge2.astype(F32)
    reach = jnp.sqrt(3.0 * dot(jnp.ones((8, CHANNELS), BF16), squares.astype(BF16), NT)[0:1, :])
    guess = bias_row * sigmoid(bias_row) * (2.0 / 3.0)
    for side in (bias_row + reach, bias_row - reach):
        guess = guess + side * sigmoid(side) * (1.0 / 6.0)
    charge = (charge_pre * sigmoid(charge_pre) - guess) * live_col
    own_total = jnp.broadcast_to(jnp.sum(charge, axis=0, keepdims=True), (8, 128))
    own_count = jnp.broadcast_to(jnp.sum(live_col, axis=0, keepdims=True), (8, 128))
    z_c = trig[4]
    z_s = trig[5]
    y_c = [jnp.broadcast_to(trig[2, m : m + 1, :], (8, ATOMS)) for m in range(TOP + 1)]
    y_s = [jnp.broadcast_to(trig[3, m : m + 1, :], (8, ATOMS)) for m in range(TOP + 1)]

    def put_wave(group, c, s):
        tile, row = group // GROUPS, (group % GROUPS) * 8
        wave_f[tile, row : row + 8, 0:ATOMS] = c
        wave_f[tile, row : row + 8, ATOMS : 2 * ATOMS] = s

    for kx in range(-TOP, TOP + 1):
        x_c = trig[0, abs(kx) : abs(kx) + 1, :]
        x_s = trig[1, abs(kx) : abs(kx) + 1, :]
        if kx < 0:
            x_s = -x_s
        xz_c = x_c * z_c - x_s * z_s
        xz_s = x_c * z_s + x_s * z_c
        base = (kx + TOP) * SIDE + TOP
        put_wave(base, xz_c, xz_s)
        for ky in range(1, TOP + 1):
            cc, ss = xz_c * y_c[ky], xz_s * y_s[ky]
            cs, sc = xz_c * y_s[ky], xz_s * y_c[ky]
            put_wave(base + ky, cc - ss, cs + sc)
            put_wave(base - ky, cc + ss, sc - cs)
    for group in range(SIDE * SIDE, SLOTS // 8):
        put_wave(group, jnp.zeros((8, ATOMS), F32), jnp.zeros((8, ATOMS), F32))

    half = iota((ATOMS, ATOMS), 1) < 64
    q_h, q_l = split(
        jnp.concatenate([jnp.where(half, charge, 0.0), jnp.where(half, 0.0, charge)], axis=0)
    )
    acc[0:128, :] = jnp.zeros((128, 128), F32)
    acc[128:256, :] = jnp.zeros((128, 128), F32)
    acc[0:8, :] = z_c * live_row
    acc[64:72, :] = z_s * live_row
    acc[128:136, :] = -(z_s * live_row)
    acc[192:200, :] = z_c * live_row
    live_rhs = jnp.concatenate(
        [jnp.transpose(acc[0:128, :]), jnp.transpose(acc[128:256, :])], axis=0
    )
    l_h, l_l = split(live_rhs)
    both_h = jnp.concatenate([q_h, l_h], axis=1)
    both_l = jnp.concatenate([q_l, l_l], axis=1)
    spare = lax.rem(iota((ROWS, 128), 0), 8) == 7


    def shift(axis, stage, kind, buffer, source, before, after, width):
        ring = []
        for side, distance in ((0, 1), (1, EDGE - 1)):
            start = before if side == 0 else after
            tag = (kind, stage, side)
            ring.append(
                send(
                    buffer.at[pl.ds(source, width)] if width > 1 else buffer.at[source],
                    buffer.at[pl.ds(start, width)] if width > 1 else buffer.at[start],
                    hsend.at[tag],
                    hrecv.at[tag],
                    cell_at(axis, distance),
                )
            )
        return ring

    def halo(stage, kind, buffer):
        if stage == 0:
            return shift(2, 0, kind, buffer, 13, 12, 14, 1)
        if stage == 1:
            return shift(0, 1, kind, buffer, 12, 9, 15, 3)
        column = (1, 0, 2)[stage - 2] * 3
        return shift(1, stage, kind, buffer, 9 + column, column, 18 + column, 3)

    lane8 = iota((8, 128), 1)
    row8 = iota((8, 128), 0)
    moved = pltpu.roll(own_total, 8, axis=1)
    extra = jnp.where(
        lane8 < 8,
        0.0,
        jnp.where(
            lane8 < 64,
            own_total,
            jnp.where(
                lane8 < 72,
                0.0,
                jnp.where(lane8 < 80, moved, jnp.where(lane8 == 80, own_count, 0.0)),
            ),
        ),
    )[0:1, :]
    tiles = []
    order = (4, 3, 5, 2, 6, 1, 7, 0)
    for step, d in enumerate(order):
        t = tile_at(d)
        w_h, w_l = split(wave_f[t])
        wave_h[t] = w_h
        wave_l[t] = w_l
        sums = dot3(w_h, w_l, both_h, both_l)
        part1[t] = jnp.where(spare, sums[:, 128:256] + extra, sums[:, 0:128]).astype(BF16)
        if step == len(order) // 2 - 1:
            pl.semaphore_wait(barrier, 3 * (EDGE - 1) + 4)
            for early in order[:step]:
                tiles.append(send_tile(0, part1, gotz1, early))
        if step >= len(order) // 2 - 1 and d > 0:
            tiles.append(send_tile(0, part1, gotz1, d))
    halo_f = halo(0, 0, nfeat)

    for load in loads[4:]:
        load.wait()
    k_h, k_l = split(kf_ref[...])
    kf2 = jnp.concatenate([k_h, k_l], axis=0)
    kx, ky, kz = kidx_ref[0:1, :], kidx_ref[1:2, :], kidx_ref[2:3, :]
    sign = jnp.where(kz < 0, -1, 1)
    slot = ((kx * sign + TOP) * SIDE + (ky * sign + TOP)) * 8 + kz * sign
    scale = 4.0 / math.sqrt(ATOMS * EDGE * EDGE * EDGE * WAVES)

    @pl.loop(0, TILES)
    def _(t):
        hot = jnp.where(iota((ROWS, WAVES), 0) + t * ROWS == slot, 1.0, 0.0).astype(BF16)
        part = dot(hot, kf2, NT)
        filt[t] = (part + pltpu.roll(part, 64, axis=1)) * scale

    for axis in range(3):
        pcol[axis] = jnp.transpose(jnp.broadcast_to(pos_ref[axis], (ATOMS, ATOMS)))
    acc[0:ATOMS, :] = jnp.zeros((ATOMS, CHANNELS), F32)
    for b in range(BASES):
        wcat[:, b * CHANNELS : b * CHANNELS + CHANNELS] = wproj_ref[b]

    def pair(q, oz, row0, rows):
        digits = nfeat[q * 3 + oz, ATOMS : ATOMS + 16, :].astype(F32)
        where = digits[0:3, :] + (digits[3:6, :] + digits[6:9, :])
        shift_y = (q // 3 - 1).astype(F32)
        shift_x = (lax.rem(q, 3) - 1).astype(F32)
        dx = (where[0:1, :] + shift_x) - pcol[0, row0 : row0 + rows, :]
        dy = (where[1:2, :] + shift_y) - pcol[1, row0 : row0 + rows, :]
        dz = (where[2:3, :] + float(oz - 1)) - pcol[2, row0 : row0 + rows, :]
        scaled = (dx * dx + dy * dy + dz * dz) * (1.0 / CUTOFF2)
        base = jnp.maximum(1.0 - scaled, 0.0)
        if oz == 1:
            same = iota((rows, ATOMS), 0) + row0 == iota((rows, ATOMS), 1)
            base = base * jnp.where(same, jnp.where(q == 4, 0.0, 1.0), 1.0)
        e1 = jnp.exp(-scaled)
        e2 = e1 * e1
        e3 = e2 * e1
        e4 = e2 * e2
        e8 = e4 * e4
        e20 = e8 * e8 * e4
        return dx, dy, dz, base, (e1, e3, e8, e20)

    STRIP = 32

    def message_block(q):
        for oz in range(3):
            for row0 in range(0, ATOMS, STRIP):
                _, _, _, base, decay = pair(q, oz, row0, STRIP)
                envelope = base * base
                for b in range(BASES):
                    column = (oz * BASES + b) * ATOMS
                    rad[row0 : row0 + STRIP, column : column + ATOMS] = (
                        decay[b] * envelope
                    ).astype(BF16)
            values = dot(nfeat[q * 3 + oz, 0:ATOMS, :], wcat[...]).astype(BF16)
            for b in range(BASES):
                nbasis[q * 3 + oz, b * ATOMS : b * ATOMS + ATOMS, :] = values[
                    :, b * CHANNELS : b * CHANNELS + CHANNELS
                ]
        near = nbasis[pl.ds(q * 3, 3)].reshape(3 * BASES * ATOMS, CHANNELS)
        acc[0:ATOMS, :] += dot(rad[...], near)

    state = {"halo": halo_f}

    def hook1(step):
        if step == 0:
            arrive(state["halo"])
            state["halo"] = halo(1, 0, nfeat)
            message_block(jnp.int32(4))
        elif step == 1:
            arrive(state["halo"])
            state["halo"] = halo(2, 0, nfeat)
            state["more"] = halo(3, 0, nfeat)
            message_block(jnp.int32(3))
            message_block(jnp.int32(5))
        elif step == 2:
            arrive(state["halo"])
            message_block(jnp.int32(1))
            message_block(jnp.int32(7))
        else:
            last = halo(4, 0, nfeat)
            arrive(state["more"])
            message_block(jnp.int32(0))
            message_block(jnp.int32(6))
            arrive(last)
            message_block(jnp.int32(2))
            message_block(jnp.int32(8))

    def neutralise(value):
        row0 = jnp.broadcast_to(value[7:8, :], (8, 128))
        total = jnp.where(lane8 < 8, pltpu.roll(row0, 56, axis=1), row0)
        total = jnp.where(lane8 < 64, total, pltpu.roll(total, 64, axis=1))
        count = jnp.sum(jnp.where(lane8 == 80, row0, 0.0), axis=1, keepdims=True)
        state["mean"] = (total / count)[0:1, :]
        parts = []
        for g in range(0, SUB, 8):
            tile = value[g : g + 8, :]
            live = jnp.broadcast_to(tile[7:8, :], (8, 128))
            live_c = jnp.sum(jnp.where(lane8 == row8, live, 0.0), axis=1, keepdims=True)
            live_s = jnp.sum(jnp.where(lane8 == row8 + 64, live, 0.0), axis=1, keepdims=True)
            parts.append(tile - jnp.where(lane8 < 64, live_c, live_s) * state["mean"])
        return jnp.concatenate(parts, axis=0)

    out_z = reduce_gather(
        0, tiles, part1, gotz1, mid1, goty1, low1, gotx1, up1, full1, neutralise, hook1
    )
    mean = state["mean"]

    pre_near = dot(acc[0:ATOMS, :].astype(BF16), wmix_ref[...])
    uv[:, CHANNELS : 2 * CHANNELS] = nbasis[13]

    prod[0:128, 0:256] = jnp.zeros((128, 256), F32)
    for d in range(EDGE):
        if d > 0:
            arrive([copies[d - 1] for copies in out_z])
        t = tile_at(EDGE - d)
        f_h, f_l = split(filt[t] * full1[t].astype(F32))
        fs_h[t] = f_h
        fs_l[t] = f_l
        prod[0:128, 0:256] += dot3(f_h, f_l, wave_h[t], wave_l[t], TN)

    potential = prod[0:64, 0:128] + prod[64:128, 128:256]
    pre = pre_near + dot(potential.astype(BF16), wlong_ref[...], TN)
    gate = sigmoid(pre)
    refined = own.astype(F32) + pre * gate
    outer = sigmoid(refined)
    readout = wenergy_ref[...]
    grad_new = live_col * readout * (outer * (1.0 + refined * (1.0 - outer)))
    grad_pre = (grad_new * (gate * (1.0 + pre * (1.0 - gate)))).astype(BF16)
    adjoint = dot(grad_pre, wmix_ref[...], NT).astype(BF16)
    nadj[13] = adjoint
    wlong2 = jnp.concatenate([wlong_ref[...], wlong_ref[...]], axis=0)
    pull_rows = dot(grad_pre, wlong2, NT)
    p_h, p_l = split(
        jnp.concatenate(
            [jnp.where(half, pull_rows, 0.0), jnp.where(half, 0.0, pull_rows)], axis=0
        )
    )

    tiles = []
    for d in (4, 3, 5, 2, 6, 1, 7, 0):
        t = tile_at(d)
        part2[t] = dot3(wave_h[t], wave_l[t], p_h, p_l).astype(BF16)
        if d > 0:
            tiles.append(send_tile(1, part2, gotz2, d))
    state["halo"] = halo(0, 1, nadj)

    upd_ref[...] = refined.astype(BF16)
    energy_col = jnp.sum(refined * outer * readout, axis=1, keepdims=True)
    energy_ref[...] = (
        jnp.transpose(jnp.broadcast_to(energy_col, (ATOMS, ATOMS)))[0:1, :] * live_row
    )

    first = iota((ATOMS, ATOMS), 0) < 64
    pull_t = jnp.transpose(pull_rows)
    neutral_t = jnp.transpose((charge - mean) * live_col)
    pull[0:128, 0:128] = jnp.where(first, 0.0, pull_t)
    pull[0:128, 128:256] = jnp.where(first, pull_t, 0.0)
    pull[128:256, 0:128] = jnp.where(first, 0.0, neutral_t)
    pull[128:256, 128:256] = jnp.where(first, neutral_t, 0.0)

    for b in range(BASES):
        uv[b * ATOMS : b * ATOMS + ATOMS, 0:CHANNELS] = adjoint
    for axis in range(3):
        acc[axis * ATOMS : axis * ATOMS + ATOMS, :] = jnp.zeros((ATOMS, ATOMS), F32)

    def force_block(q):
        for oz in range(3):
            for b in range(BASES):
                rows = slice(b * ATOMS, b * ATOMS + ATOMS)
                near = jnp.concatenate([nbasis[q * 3 + oz, rows, :], nadj[q * 3 + oz]], axis=1)
                prod[rows, oz * 128 : oz * 128 + 128] = dot(uv[rows, :], near, NT)
        for row0 in range(0, ATOMS, STRIP):
            total_x = total_y = total_z = None
            for oz in range(3):
                dx, dy, dz, base, decay = pair(q, oz, row0, STRIP)
                envelope = base * base
                double = base + base
                strength = None
                for b, rate in enumerate((1.0, 3.0, 8.0, 20.0)):
                    got = prod[
                        b * ATOMS + row0 : b * ATOMS + row0 + STRIP, oz * 128 : oz * 128 + 128
                    ]
                    term = decay[b] * (envelope * rate + double) * got
                    strength = term if strength is None else strength + term
                if total_x is None:
                    total_x, total_y, total_z = strength * dx, strength * dy, strength * dz
                else:
                    total_x = total_x + strength * dx
                    total_y = total_y + strength * dy
                    total_z = total_z + strength * dz
            acc[row0 : row0 + STRIP, :] += total_x
            acc[128 + row0 : 128 + row0 + STRIP, :] += total_y
            acc[256 + row0 : 256 + row0 + STRIP, :] += total_z

    def hook2(step):
        if step != 3:
            drain()
        if step == 0:
            arrive(state["halo"])
            state["halo"] = halo(1, 1, nadj)
            force_block(jnp.int32(4))
        elif step == 1:
            arrive(state["halo"])
            state["halo"] = halo(2, 1, nadj)
            state["more"] = halo(3, 1, nadj)
            force_block(jnp.int32(3))
            force_block(jnp.int32(5))
        elif step == 2:
            arrive(state["halo"])
            force_block(jnp.int32(1))
            force_block(jnp.int32(7))
        else:
            last = halo(4, 1, nadj)
            arrive(state["more"])
            force_block(jnp.int32(0))
            force_block(jnp.int32(6))
            arrive(last)
            force_block(jnp.int32(2))
            force_block(jnp.int32(8))

    out_z = reduce_gather(
        1, tiles, part2, gotz2, mid2, goty2, low2, gotx2, up2, full2, lambda v: v, hook2
    )

    lane = iota((ATOMS, ATOMS), 1)
    columns = jnp.zeros((ATOMS, ATOMS), F32)
    for axis in range(3):
        near_sum = jnp.sum(acc[axis * ATOMS : axis * ATOMS + ATOMS, :], axis=1, keepdims=True)
        columns = jnp.where(lane == axis, near_sum, columns)
    near_force = jnp.transpose(columns)[0:8, :] * (-2.0 / CUTOFF2)
    r_h, r_l = split(pull[...])

    prod[0:8, 0:128] = jnp.zeros((8, 128), F32)
    for d in range(EDGE):
        if d > 0:
            arrive([copies[d - 1] for copies in out_z])
        t = tile_at(EDGE - d)
        b_h, b_l = split(filt[t] * full2[t].astype(F32))
        left_h = jnp.concatenate([fs_h[t], b_h], axis=1)
        left_l = jnp.concatenate([fs_l[t], b_l], axis=1)
        mixed = dot3(left_h, left_l, r_h, r_l)
        waves = wave_f[t]
        d_h, d_l = split(
            waves[:, 0:128] * mixed[:, 0:128] - waves[:, 128:256] * mixed[:, 128:256]
        )
        index = iota((8, ROWS), 1) + t * ROWS
        axis_row = iota((8, ROWS), 0)
        group = lax.shift_right_logical(index, 3)
        group_x = lax.shift_right_logical(group * 79, 10)
        value_x = group_x - TOP
        value_y = group - group_x * SIDE - TOP
        value_z = lax.bitwise_and(index, 7)
        values = jnp.where(axis_row == 0, value_x, jnp.where(axis_row == 1, value_y, value_z))
        rows = values.astype(F32).astype(BF16)
        prod[0:8, 0:128] += dot(rows, d_h) + dot(rows, d_l)

    force = near_force - prod[0:8, 0:128] * (2.0 * math.pi / EDGE)
    for axis in range(3):
        force_ref[axis] = force[axis : axis + 1, :]
    drain()


def shards(
    features,
    positions,
    counts,
    w_proj,
    w_mix,
    w_long,
    w_charge,
    charge_bias,
    w_energy,
    k_filter,
    k_index,
):
    hbm = pl.BlockSpec(memory_space=pltpu.HBM)
    vmem = pl.BlockSpec(memory_space=pltpu.VMEM)
    dma = pltpu.SemaphoreType.DMA
    def reduce_buffers(narrow_y, narrow_z):
        return [
            pltpu.VMEM((TILES, ROWS, 128), BF16),
            pltpu.VMEM((EDGE - 1, ROWS, 128), BF16),
            pltpu.VMEM((PIECES, EDGE, SUB, 128), narrow_y),
            pltpu.VMEM((EDGE - 1, PIECES, SUB, 128), narrow_y),
            pltpu.VMEM((PIECES, SUB, 128), narrow_z),
            pltpu.VMEM((EDGE - 1, PIECES, SUB, 128), narrow_z),
            pltpu.VMEM((PIECES, EDGE, SUB, 128), BF16),
            pltpu.VMEM((TILES, ROWS, 128), BF16),
        ]

    updated, energy, force = pl.pallas_call(
        block_kernel,
        name="block",
        out_shape=(
            jax.ShapeDtypeStruct((ATOMS, CHANNELS), BF16),
            jax.ShapeDtypeStruct((1, ATOMS), F32),
            jax.ShapeDtypeStruct((3, 1, ATOMS), F32),
        ),
        in_specs=[pl.BlockSpec(memory_space=pltpu.SMEM)] + [hbm] * 10,
        out_specs=(vmem, vmem, vmem),
        scratch_shapes=[
            pltpu.VMEM((ATOMS, CHANNELS), BF16),
            pltpu.VMEM((3, 1, ATOMS), F32),
            pltpu.VMEM((BASES, CHANNELS, CHANNELS), BF16),
            pltpu.VMEM((CHANNELS, CHANNELS), BF16),
            pltpu.VMEM((64, CHANNELS), BF16),
            pltpu.VMEM((64, CHANNELS), BF16),
            pltpu.VMEM((1, 64), F32),
            pltpu.VMEM((1, CHANNELS), F32),
            pltpu.VMEM((64, WAVES), F32),
            pltpu.VMEM((3, WAVES), jnp.int32),
            pltpu.VMEM((27, ATOMS + 16, CHANNELS), BF16),
            pltpu.VMEM((27, ATOMS, CHANNELS), BF16),
            pltpu.VMEM((16, ATOMS), F32),
            pltpu.VMEM((6, 8, ATOMS), F32),
            pltpu.VMEM((8, 128), F32),
            pltpu.VMEM((TILES, ROWS, 256), F32),
            pltpu.VMEM((TILES, ROWS, 256), BF16),
            pltpu.VMEM((TILES, ROWS, 256), BF16),
            pltpu.VMEM((TILES, ROWS, 128), F32),
            pltpu.VMEM((TILES, ROWS, 128), BF16),
            pltpu.VMEM((TILES, ROWS, 128), BF16),
        ]
        + reduce_buffers(BF16, F32)
        + reduce_buffers(BF16, BF16)
        + [
            pltpu.VMEM((3, ATOMS, ATOMS), F32),
            pltpu.VMEM((ATOMS, 3 * BASES * ATOMS), BF16),
            pltpu.VMEM((CHANNELS, BASES * CHANNELS), BF16),
            pltpu.VMEM((27, BASES * ATOMS, CHANNELS), BF16),
            pltpu.VMEM((BASES * ATOMS, CHANNELS), F32),
            pltpu.VMEM((BASES * ATOMS, 3 * 128), F32),
            pltpu.VMEM((BASES * ATOMS, 2 * CHANNELS), BF16),
            pltpu.VMEM((256, 256), F32),
            dma((10,)),
            dma((2, 5, PIECES, EDGE - 1)),
            dma((2, 5, PIECES, EDGE - 1)),
            dma((2, 5, 2)),
            dma((2, 5, 2)),
        ],
        compiler_params=pltpu.CompilerParams(
            collective_id=0, has_side_effects=True, vmem_limit_bytes=48 * 1024 * 1024
        ),
    )(
        counts.reshape(1),
        pltpu.with_memory_space_constraint(features[0, 0, 0], pltpu.HBM),
        pltpu.with_memory_space_constraint(positions.reshape(3, 1, ATOMS), pltpu.HBM),
        pltpu.with_memory_space_constraint(w_proj, pltpu.HBM),
        pltpu.with_memory_space_constraint(w_mix, pltpu.HBM),
        pltpu.with_memory_space_constraint(w_long, pltpu.HBM),
        pltpu.with_memory_space_constraint(w_charge, pltpu.HBM),
        pltpu.with_memory_space_constraint(charge_bias.reshape(1, 64), pltpu.HBM),
        pltpu.with_memory_space_constraint(w_energy.reshape(1, CHANNELS), pltpu.HBM),
        pltpu.with_memory_space_constraint(k_filter, pltpu.HBM),
        pltpu.with_memory_space_constraint(k_index, pltpu.HBM),
    )
    return (
        updated[None, None, None],
        energy.reshape(1, 1, 1, ATOMS),
        force.reshape(1, 1, 1, 3, ATOMS),
    )


def solution(mesh):
    cells = P("gx", "gy", "gz")
    in_specs = (cells, cells, cells) + (P(),) * 8
    return jax.shard_map(
        shards, mesh=mesh, in_specs=in_specs, out_specs=(cells, cells, cells), check_vma=False
    )
```

```python
import functools
import math

import jax
import jax.numpy as jnp
from jax import lax
from jax.experimental import pallas as pl
from jax.experimental.pallas import tpu as pltpu
from jax.sharding import PartitionSpec as P

MESH = pl.DeviceIdType.MESH
CUTOFF2 = 0.9 * 0.9
ATOMS = 128
CHANNELS = 128
BASES = 4
EDGE = 8
WAVES = 2048
TOP = 6
SIDE = 2 * TOP + 1
TILES = 8
ROWS = 176
GROUPS = 22
PIECES = 1
PIECE = 176
SUB = 24
SLOTS = TILES * ROWS
F32 = jnp.float32
BF16 = jnp.bfloat16
NT = (((1,), (1,)), ((), ()))
NN = (((1,), (0,)), ((), ()))
TN = (((0,), (0,)), ((), ()))


def dot(a, b, dims=NN):
    return lax.dot_general(a, b, dims, preferred_element_type=F32)


def split(value):
    high = value.astype(BF16)
    low = (value - high.astype(F32)).astype(BF16)
    return high, low


def dot3(a_high, a_low, b_high, b_low, dims=NN):
    return dot(a_high, b_high, dims) + dot(a_high, b_low, dims) + dot(a_low, b_high, dims)


def iota(shape, dim):
    return lax.broadcasted_iota(jnp.int32, shape, dim)


def sigmoid(v):
    return 1.0 / (1.0 + jnp.exp(-v))


def block_kernel(
    counts_ref,
    feat_hbm,
    pos_hbm,
    wproj_hbm,
    wmix_hbm,
    wlong_hbm,
    wcharge_hbm,
    bias_hbm,
    wenergy_hbm,
    kf_hbm,
    kidx_hbm,
    upd_ref,
    energy_ref,
    force_ref,
    feat_ref,
    pos_ref,
    wproj_ref,
    wmix_ref,
    wlong_ref,
    wcharge_ref,
    bias_ref,
    wenergy_ref,
    kf_ref,
    kidx_ref,
    nfeat,
    nadj,
    pack,
    trig,
    row,
    wave_f,
    wave_h,
    wave_l,
    filt,
    fs_h,
    fs_l,
    part1,
    gotz1,
    mid1,
    goty1,
    low1,
    gotx1,
    up1,
    full1,
    part2,
    gotz2,
    mid2,
    goty2,
    low2,
    gotx2,
    up2,
    full2,
    pcol,
    rad,
    wcat,
    nbasis,
    acc,
    prod,
    uv,
    pull,
    load_sem,
    send_sem,
    recv_sem,
    hsend,
    hrecv,
):
    me = tuple(lax.axis_index(name) for name in ("gx", "gy", "gz"))

    zcore, yrow, xhalf = lax.rem(me[0], 2), me[1], lax.rem(me[2], 2)
    place = ((me[0] // 2) * 2 + xhalf, yrow, (me[2] // 2) * 2 + zcore)

    def device_at(axis, distance):
        peer = lax.rem(place[axis] + distance, EDGE)
        high, low = (peer // 2) * 2, lax.rem(peer, 2)
        if axis == 0:
            return peer, (high + zcore, me[1], (me[2] // 2) * 2 + low)
        if axis == 1:
            return peer, (me[0], peer, me[2])
        return peer, ((me[0] // 2) * 2 + low, me[1], high + xhalf)

    def cell_at(axis, distance):
        coords = list(me)
        coords[axis] = lax.rem(me[axis] + distance, EDGE)
        return tuple(coords)

    loads = [
        pltpu.make_async_copy(source, target, load_sem.at[i])
        for i, (source, target) in enumerate(
            (
                (pos_hbm, pos_ref),
                (feat_hbm, feat_ref),
                (wcharge_hbm, wcharge_ref),
                (bias_hbm, bias_ref),
                (kidx_hbm, kidx_ref),
                (kf_hbm, kf_ref),
                (wproj_hbm, wproj_ref),
                (wmix_hbm, wmix_ref),
                (wlong_hbm, wlong_ref),
                (wenergy_hbm, wenergy_ref),
            )
        )
    ]
    for load in loads:
        load.start()
    barrier = pltpu.get_barrier_semaphore()
    for axis in range(3):
        for d in range(1, EDGE):
            pl.semaphore_signal(
                barrier, inc=1, device_id=device_at(axis, d)[1], device_id_type=MESH
            )

    for axis in (0, 2):
        for d in (1, EDGE - 1):
            pl.semaphore_signal(
                barrier, inc=1, device_id=cell_at(axis, d), device_id_type=MESH
            )

    sent = []

    def drain():
        for copy in sent:
            copy.wait_send()
        sent.clear()

    def send(src, dst, ssem, rsem, device):
        copy = pltpu.make_async_remote_copy(
            src_ref=src,
            dst_ref=dst,
            send_sem=ssem,
            recv_sem=rsem,
            device_id=device,
            device_id_type=MESH,
        )
        copy.start()
        sent.append(copy)
        return copy

    def spread(axis, slot, source, target):
        copies = []
        for d in range(1, EDGE):
            peer, device = device_at(axis, d)
            copies.append(
                send(
                    source(peer),
                    target(d - 1),
                    send_sem.at[slot + (d - 1,)],
                    recv_sem.at[slot + (d - 1,)],
                    device,
                )
            )
        return copies

    def arrive(copies):
        for copy in copies:
            copy.wait_recv()

    def tile_at(distance):
        return lax.rem(place[2] + distance, EDGE)

    def send_tile(kind, part, gotz, d):
        peer, device = device_at(2, d)
        copies = []
        for p in range(PIECES):
            rows = pl.ds(p * PIECE, PIECE)
            copies.append(
                send(
                    part.at[peer, rows],
                    gotz.at[d - 1, rows],
                    send_sem.at[kind, 0, p, d - 1],
                    recv_sem.at[kind, 0, p, d - 1],
                    device,
                )
            )
        return copies

    def reduce_gather(kind, tiles, part, gotz, mid, goty, low, gotx, up, full, finish, hook):
        stages = []
        for p in range(PIECES):
            arrive([copies[p] for copies in tiles])
            rows = slice(p * PIECE, p * PIECE + PIECE)
            value = part[place[2], rows, :].astype(F32)
            for d in range(1, EDGE):
                value = value + gotz[d - 1, rows, :].astype(F32)
            for c in range(EDGE):
                rows = value[c * SUB : min(c * SUB + SUB, PIECE), :]
                short = SUB - rows.shape[0]
                if short:
                    rows = jnp.concatenate([rows, jnp.zeros((short, 128), F32)], axis=0)
                mid[p, c] = rows.astype(mid.dtype)
            stages.append(
                spread(
                    1, (kind, 1, p), lambda peer: mid.at[p, peer], lambda s: goty.at[s, p]
                )
            )
        hook(0)
        copies, stages = stages, []
        for p in range(PIECES):
            arrive(copies[p])
            value = mid[p, place[1]].astype(F32)
            for d in range(1, EDGE):
                value = value + goty[d - 1, p].astype(F32)
            low[p] = value.astype(low.dtype)
            stages.append(
                spread(0, (kind, 2, p), lambda peer: low.at[p], lambda s: gotx.at[s, p])
            )
        hook(1)
        copies, stages = stages, []
        for p in range(PIECES):
            arrive(copies[p])
            value = low[p].astype(F32)
            for d in range(1, EDGE):
                value = value + gotx[d - 1, p].astype(F32)
            up[p, place[1]] = finish(value).astype(BF16)
            stages.append(
                spread(
                    1, (kind, 3, p), lambda peer: up.at[p, place[1]], lambda s: up.at[p, place[1]]
                )
            )
        hook(2)
        copies, stages = stages, []
        for p in range(PIECES):
            arrive(copies[p])
            rows = pl.ds(p * PIECE, PIECE)
            full[place[2], p * PIECE : p * PIECE + PIECE, :] = jnp.concatenate(
                [
                    up[p, c, 0 : min(SUB, PIECE - c * SUB), :].astype(F32)
                    for c in range(EDGE)
                ],
                axis=0,
            ).astype(BF16)
            stages.append(
                spread(
                    2,
                    (kind, 4, p),
                    lambda peer: full.at[place[2], rows],
                    lambda s: full.at[place[2], rows],
                )
            )
        hook(3)
        return stages

    live_row = (iota((1, ATOMS), 1) < counts_ref[0]).astype(F32)
    live_col = (iota((ATOMS, CHANNELS), 0) < counts_ref[0]).astype(F32)
    row[...] = jnp.zeros((8, 128), F32)
    pack[...] = jnp.zeros((16, 128), F32)
    loads[0].wait()

    steps = iota((8, ATOMS), 0).astype(F32)
    for axis in range(3):
        unit = (pos_ref[axis] + me[axis].astype(F32)) * (1.0 / EDGE)
        orders = steps if axis < 2 else jnp.where(steps > 6.5, 0.0, steps)
        turns = orders * unit
        angle = (turns - jnp.floor(turns + 0.5)) * (2.0 * math.pi)
        trig[2 * axis] = jnp.cos(angle)
        trig[2 * axis + 1] = jnp.sin(angle)
    loads[1].wait()
    loads[2].wait()
    loads[3].wait()
    own = feat_ref[...]
    masked = own * live_col.astype(BF16)
    nfeat[13, 0:ATOMS, :] = masked
    for axis in range(3):
        rest = pos_ref[axis]
        for step in range(3):
            digit = rest.astype(BF16).astype(F32)
            pack[3 * step + axis : 3 * step + axis + 1, :] = digit
            rest = rest - digit
    nfeat[13, ATOMS : ATOMS + 16, :] = pack[...].astype(BF16)

    wcharge2 = jnp.concatenate([wcharge_ref[...], wcharge_ref[...]], axis=0)
    row[0:1, 0:64] = bias_ref[...]
    bias = row[...]
    bias_row = (bias + pltpu.roll(bias, 64, axis=1))[0:1, :]
    charge_pre = dot(masked, wcharge2, NT) + bias_row
    squares = wcharge2.astype(F32) * wcharge2.astype(F32)
    reach = jnp.sqrt(3.0 * dot(jnp.ones((8, CHANNELS), BF16), squares.astype(BF16), NT)[0:1, :])
    guess = bias_row * sigmoid(bias_row) * (2.0 / 3.0)
    for side in (bias_row + reach, bias_row - reach):
        guess = guess + side * sigmoid(side) * (1.0 / 6.0)
    charge = (charge_pre * sigmoid(charge_pre) - guess) * live_col
    own_total = jnp.broadcast_to(jnp.sum(charge, axis=0, keepdims=True), (8, 128))
    own_count = jnp.broadcast_to(jnp.sum(live_col, axis=0, keepdims=True), (8, 128))
    z_c = trig[4]
    z_s = trig[5]
    y_c = [jnp.broadcast_to(trig[2, m : m + 1, :], (8, ATOMS)) for m in range(TOP + 1)]
    y_s = [jnp.broadcast_to(trig[3, m : m + 1, :], (8, ATOMS)) for m in range(TOP + 1)]

    def put_wave(group, c, s):
        tile, row = group // GROUPS, (group % GROUPS) * 8
        wave_f[tile, row : row + 8, 0:ATOMS] = c
        wave_f[tile, row : row + 8, ATOMS : 2 * ATOMS] = s

    for kx in range(-TOP, TOP + 1):
        x_c = trig[0, abs(kx) : abs(kx) + 1, :]
        x_s = trig[1, abs(kx) : abs(kx) + 1, :]
        if kx < 0:
            x_s = -x_s
        xz_c = x_c * z_c - x_s * z_s
        xz_s = x_c * z_s + x_s * z_c
        base = (kx + TOP) * SIDE + TOP
        put_wave(base, xz_c, xz_s)
        for ky in range(1, TOP + 1):
            cc, ss = xz_c * y_c[ky], xz_s * y_s[ky]
            cs, sc = xz_c * y_s[ky], xz_s * y_c[ky]
            put_wave(base + ky, cc - ss, cs + sc)
            put_wave(base - ky, cc + ss, sc - cs)
    for group in range(SIDE * SIDE, SLOTS // 8):
        put_wave(group, jnp.zeros((8, ATOMS), F32), jnp.zeros((8, ATOMS), F32))

    half = iota((ATOMS, ATOMS), 1) < 64
    q_h, q_l = split(
        jnp.concatenate([jnp.where(half, charge, 0.0), jnp.where(half, 0.0, charge)], axis=0)
    )
    acc[0:128, :] = jnp.zeros((128, 128), F32)
    acc[128:256, :] = jnp.zeros((128, 128), F32)
    acc[0:8, :] = z_c * live_row
    acc[64:72, :] = z_s * live_row
    acc[128:136, :] = -(z_s * live_row)
    acc[192:200, :] = z_c * live_row
    live_rhs = jnp.concatenate(
        [jnp.transpose(acc[0:128, :]), jnp.transpose(acc[128:256, :])], axis=0
    )
    l_h, l_l = split(live_rhs)
    both_h = jnp.concatenate([q_h, l_h], axis=1)
    both_l = jnp.concatenate([q_l, l_l], axis=1)
    spare = lax.rem(iota((ROWS, 128), 0), 8) == 7


    def shift(axis, stage, kind, buffer, source, before, after, width):
        ring = []
        for side, distance in ((0, 1), (1, EDGE - 1)):
            start = before if side == 0 else after
            tag = (kind, stage, side)
            ring.append(
                send(
                    buffer.at[pl.ds(source, width)] if width > 1 else buffer.at[source],
                    buffer.at[pl.ds(start, width)] if width > 1 else buffer.at[start],
                    hsend.at[tag],
                    hrecv.at[tag],
                    cell_at(axis, distance),
                )
            )
        return ring

    def halo(stage, kind, buffer):
        if stage == 0:
            return shift(2, 0, kind, buffer, 13, 12, 14, 1)
        if stage == 1:
            return shift(0, 1, kind, buffer, 12, 9, 15, 3)
        column = (1, 0, 2)[stage - 2] * 3
        return shift(1, stage, kind, buffer, 9 + column, column, 18 + column, 3)

    lane8 = iota((8, 128), 1)
    row8 = iota((8, 128), 0)
    moved = pltpu.roll(own_total, 8, axis=1)
    extra = jnp.where(
        lane8 < 8,
        0.0,
        jnp.where(
            lane8 < 64,
            own_total,
            jnp.where(
                lane8 < 72,
                0.0,
                jnp.where(lane8 < 80, moved, jnp.where(lane8 == 80, own_count, 0.0)),
            ),
        ),
    )[0:1, :]
    tiles = []
    order = (4, 3, 5, 2, 6, 1, 7, 0)
    for step, d in enumerate(order):
        t = tile_at(d)
        w_h, w_l = split(wave_f[t])
        wave_h[t] = w_h
        wave_l[t] = w_l
        sums = dot3(w_h, w_l, both_h, both_l)
        part1[t] = jnp.where(spare, sums[:, 128:256] + extra, sums[:, 0:128]).astype(BF16)
        if step == len(order) // 2 - 1:
            pl.semaphore_wait(barrier, 3 * (EDGE - 1) + 4)
            for early in order[:step]:
                tiles.append(send_tile(0, part1, gotz1, early))
        if step >= len(order) // 2 - 1 and d > 0:
            tiles.append(send_tile(0, part1, gotz1, d))
    halo_f = halo(0, 0, nfeat)

    for load in loads[4:]:
        load.wait()
    k_h, k_l = split(kf_ref[...])
    kf2 = jnp.concatenate([k_h, k_l], axis=0)
    kx, ky, kz = kidx_ref[0:1, :], kidx_ref[1:2, :], kidx_ref[2:3, :]
    sign = jnp.where(kz < 0, -1, 1)
    slot = ((kx * sign + TOP) * SIDE + (ky * sign + TOP)) * 8 + kz * sign
    scale = 4.0 / math.sqrt(ATOMS * EDGE * EDGE * EDGE * WAVES)

    @pl.loop(0, TILES)
    def _(t):
        hot = jnp.where(iota((ROWS, WAVES), 0) + t * ROWS == slot, 1.0, 0.0).astype(BF16)
        part = dot(hot, kf2, NT)
        filt[t] = (part + pltpu.roll(part, 64, axis=1)) * scale

    for axis in range(3):
        pcol[axis] = jnp.transpose(jnp.broadcast_to(pos_ref[axis], (ATOMS, ATOMS)))
    acc[0:ATOMS, :] = jnp.zeros((ATOMS, CHANNELS), F32)
    for b in range(BASES):
        wcat[:, b * CHANNELS : b * CHANNELS + CHANNELS] = wproj_ref[b]

    def pair(q, oz, row0, rows):
        digits = nfeat[q * 3 + oz, ATOMS : ATOMS + 16, :].astype(F32)
        where = digits[0:3, :] + (digits[3:6, :] + digits[6:9, :])
        shift_y = (q // 3 - 1).astype(F32)
        shift_x = (lax.rem(q, 3) - 1).astype(F32)
        dx = (where[0:1, :] + shift_x) - pcol[0, row0 : row0 + rows, :]
        dy = (where[1:2, :] + shift_y) - pcol[1, row0 : row0 + rows, :]
        dz = (where[2:3, :] + float(oz - 1)) - pcol[2, row0 : row0 + rows, :]
        scaled = (dx * dx + dy * dy + dz * dz) * (1.0 / CUTOFF2)
        base = jnp.maximum(1.0 - scaled, 0.0)
        if oz == 1:
            same = iota((rows, ATOMS), 0) + row0 == iota((rows, ATOMS), 1)
            base = base * jnp.where(same, jnp.where(q == 4, 0.0, 1.0), 1.0)
        e1 = jnp.exp(-scaled)
        e2 = e1 * e1
        e3 = e2 * e1
        e4 = e2 * e2
        e8 = e4 * e4
        e20 = e8 * e8 * e4
        return dx, dy, dz, base, (e1, e3, e8, e20)

    STRIP = 32

    def message_block(q):
        for oz in range(3):
            for row0 in range(0, ATOMS, STRIP):
                _, _, _, base, decay = pair(q, oz, row0, STRIP)
                envelope = base * base
                for b in range(BASES):
                    column = (oz * BASES + b) * ATOMS
                    rad[row0 : row0 + STRIP, column : column + ATOMS] = (
                        decay[b] * envelope
                    ).astype(BF16)
            values = dot(nfeat[q * 3 + oz, 0:ATOMS, :], wcat[...]).astype(BF16)
            for b in range(BASES):
                nbasis[q * 3 + oz, b * ATOMS : b * ATOMS + ATOMS, :] = values[
                    :, b * CHANNELS : b * CHANNELS + CHANNELS
                ]
        near = nbasis[pl.ds(q * 3, 3)].reshape(3 * BASES * ATOMS, CHANNELS)
        acc[0:ATOMS, :] += dot(rad[...], near)

    state = {"halo": halo_f}

    def hook1(step):
        if step == 0:
            arrive(state["halo"])
            state["halo"] = halo(1, 0, nfeat)
            message_block(jnp.int32(4))
        elif step == 1:
            arrive(state["halo"])
            state["halo"] = halo(2, 0, nfeat)
            state["more"] = halo(3, 0, nfeat)
            message_block(jnp.int32(3))
            message_block(jnp.int32(5))
        elif step == 2:
            arrive(state["halo"])
            message_block(jnp.int32(1))
            message_block(jnp.int32(7))
        else:
            last = halo(4, 0, nfeat)
            arrive(state["more"])
            message_block(jnp.int32(0))
            message_block(jnp.int32(6))
            arrive(last)
            message_block(jnp.int32(2))
            message_block(jnp.int32(8))

    def neutralise(value):
        row0 = jnp.broadcast_to(value[7:8, :], (8, 128))
        total = jnp.where(lane8 < 8, pltpu.roll(row0, 56, axis=1), row0)
        total = jnp.where(lane8 < 64, total, pltpu.roll(total, 64, axis=1))
        count = jnp.sum(jnp.where(lane8 == 80, row0, 0.0), axis=1, keepdims=True)
        state["mean"] = (total / count)[0:1, :]
        parts = []
        for g in range(0, SUB, 8):
            tile = value[g : g + 8, :]
            live = jnp.broadcast_to(tile[7:8, :], (8, 128))
            live_c = jnp.sum(jnp.where(lane8 == row8, live, 0.0), axis=1, keepdims=True)
            live_s = jnp.sum(jnp.where(lane8 == row8 + 64, live, 0.0), axis=1, keepdims=True)
            parts.append(tile - jnp.where(lane8 < 64, live_c, live_s) * state["mean"])
        return jnp.concatenate(parts, axis=0)

    out_z = reduce_gather(
        0, tiles, part1, gotz1, mid1, goty1, low1, gotx1, up1, full1, neutralise, hook1
    )
    mean = state["mean"]

    pre_near = dot(acc[0:ATOMS, :].astype(BF16), wmix_ref[...])
    uv[:, CHANNELS : 2 * CHANNELS] = nbasis[13]

    prod[0:128, 0:256] = jnp.zeros((128, 256), F32)
    for d in range(EDGE):
        if d > 0:
            arrive([copies[d - 1] for copies in out_z])
        t = tile_at(EDGE - d)
        f_h, f_l = split(filt[t] * full1[t].astype(F32))
        fs_h[t] = f_h
        fs_l[t] = f_l
        prod[0:128, 0:256] += dot3(f_h, f_l, wave_h[t], wave_l[t], TN)

    potential = prod[0:64, 0:128] + prod[64:128, 128:256]
    pre = pre_near + dot(potential.astype(BF16), wlong_ref[...], TN)
    gate = sigmoid(pre)
    refined = own.astype(F32) + pre * gate
    outer = sigmoid(refined)
    readout = wenergy_ref[...]
    grad_new = live_col * readout * (outer * (1.0 + refined * (1.0 - outer)))
    grad_pre = (grad_new * (gate * (1.0 + pre * (1.0 - gate)))).astype(BF16)
    adjoint = dot(grad_pre, wmix_ref[...], NT).astype(BF16)
    nadj[13] = adjoint
    wlong2 = jnp.concatenate([wlong_ref[...], wlong_ref[...]], axis=0)
    pull_rows = dot(grad_pre, wlong2, NT)
    p_h, p_l = split(
        jnp.concatenate(
            [jnp.where(half, pull_rows, 0.0), jnp.where(half, 0.0, pull_rows)], axis=0
        )
    )

    tiles = []
    for d in (4, 3, 5, 2, 6, 1, 7, 0):
        t = tile_at(d)
        part2[t] = dot3(wave_h[t], wave_l[t], p_h, p_l).astype(BF16)
        if d > 0:
            tiles.append(send_tile(1, part2, gotz2, d))
    state["halo"] = halo(0, 1, nadj)

    upd_ref[...] = refined.astype(BF16)
    energy_col = jnp.sum(refined * outer * readout, axis=1, keepdims=True)
    energy_ref[...] = (
        jnp.transpose(jnp.broadcast_to(energy_col, (ATOMS, ATOMS)))[0:1, :] * live_row
    )

    first = iota((ATOMS, ATOMS), 0) < 64
    pull_t = jnp.transpose(pull_rows)
    neutral_t = jnp.transpose((charge - mean) * live_col)
    pull[0:128, 0:128] = jnp.where(first, 0.0, pull_t)
    pull[0:128, 128:256] = jnp.where(first, pull_t, 0.0)
    pull[128:256, 0:128] = jnp.where(first, 0.0, neutral_t)
    pull[128:256, 128:256] = jnp.where(first, neutral_t, 0.0)

    for b in range(BASES):
        uv[b * ATOMS : b * ATOMS + ATOMS, 0:CHANNELS] = adjoint
    for axis in range(3):
        acc[axis * ATOMS : axis * ATOMS + ATOMS, :] = jnp.zeros((ATOMS, ATOMS), F32)

    def force_block(q):
        for oz in range(3):
            for b in range(BASES):
                rows = slice(b * ATOMS, b * ATOMS + ATOMS)
                near = jnp.concatenate([nbasis[q * 3 + oz, rows, :], nadj[q * 3 + oz]], axis=1)
                prod[rows, oz * 128 : oz * 128 + 128] = dot(uv[rows, :], near, NT)
        for row0 in range(0, ATOMS, STRIP):
            total_x = total_y = total_z = None
            for oz in range(3):
                dx, dy, dz, base, decay = pair(q, oz, row0, STRIP)
                envelope = base * base
                double = base + base
                strength = None
                for b, rate in enumerate((1.0, 3.0, 8.0, 20.0)):
                    got = prod[
                        b * ATOMS + row0 : b * ATOMS + row0 + STRIP, oz * 128 : oz * 128 + 128
                    ]
                    term = decay[b] * (envelope * rate + double) * got
                    strength = term if strength is None else strength + term
                if total_x is None:
                    total_x, total_y, total_z = strength * dx, strength * dy, strength * dz
                else:
                    total_x = total_x + strength * dx
                    total_y = total_y + strength * dy
                    total_z = total_z + strength * dz
            acc[row0 : row0 + STRIP, :] += total_x
            acc[128 + row0 : 128 + row0 + STRIP, :] += total_y
            acc[256 + row0 : 256 + row0 + STRIP, :] += total_z

    def hook2(step):
        if step != 3:
            drain()
        if step == 0:
            arrive(state["halo"])
            state["halo"] = halo(1, 1, nadj)
            force_block(jnp.int32(4))
        elif step == 1:
            arrive(state["halo"])
            state["halo"] = halo(2, 1, nadj)
            state["more"] = halo(3, 1, nadj)
            force_block(jnp.int32(3))
            force_block(jnp.int32(5))
        elif step == 2:
            arrive(state["halo"])
            force_block(jnp.int32(1))
            force_block(jnp.int32(7))
        else:
            last = halo(4, 1, nadj)
            arrive(state["more"])
            force_block(jnp.int32(0))
            force_block(jnp.int32(6))
            arrive(last)
            force_block(jnp.int32(2))
            force_block(jnp.int32(8))

    out_z = reduce_gather(
        1, tiles, part2, gotz2, mid2, goty2, low2, gotx2, up2, full2, lambda v: v, hook2
    )

    lane = iota((ATOMS, ATOMS), 1)
    columns = jnp.zeros((ATOMS, ATOMS), F32)
    for axis in range(3):
        near_sum = jnp.sum(acc[axis * ATOMS : axis * ATOMS + ATOMS, :], axis=1, keepdims=True)
        columns = jnp.where(lane == axis, near_sum, columns)
    near_force = jnp.transpose(columns)[0:8, :] * (-2.0 / CUTOFF2)
    r_h, r_l = split(pull[...])

    prod[0:8, 0:128] = jnp.zeros((8, 128), F32)
    for d in range(EDGE):
        if d > 0:
            arrive([copies[d - 1] for copies in out_z])
        t = tile_at(EDGE - d)
        b_h, b_l = split(filt[t] * full2[t].astype(F32))
        left_h = jnp.concatenate([fs_h[t], b_h], axis=1)
        left_l = jnp.concatenate([fs_l[t], b_l], axis=1)
        mixed = dot3(left_h, left_l, r_h, r_l)
        waves = wave_f[t]
        d_h, d_l = split(
            waves[:, 0:128] * mixed[:, 0:128] - waves[:, 128:256] * mixed[:, 128:256]
        )
        index = iota((8, ROWS), 1) + t * ROWS
        axis_row = iota((8, ROWS), 0)
        group = lax.shift_right_logical(index, 3)
        group_x = lax.shift_right_logical(group * 79, 10)
        value_x = group_x - TOP
        value_y = group - group_x * SIDE - TOP
        value_z = lax.bitwise_and(index, 7)
        values = jnp.where(axis_row == 0, value_x, jnp.where(axis_row == 1, value_y, value_z))
        rows = values.astype(F32).astype(BF16)
        prod[0:8, 0:128] += dot(rows, d_h) + dot(rows, d_l)

    force = near_force - prod[0:8, 0:128] * (2.0 * math.pi / EDGE)
    for axis in range(3):
        force_ref[axis] = force[axis : axis + 1, :]
    drain()


def shards(
    features,
    positions,
    counts,
    w_proj,
    w_mix,
    w_long,
    w_charge,
    charge_bias,
    w_energy,
    k_filter,
    k_index,
):
    hbm = pl.BlockSpec(memory_space=pltpu.HBM)
    vmem = pl.BlockSpec(memory_space=pltpu.VMEM)
    dma = pltpu.SemaphoreType.DMA
    def reduce_buffers(narrow_y, narrow_z):
        return [
            pltpu.VMEM((TILES, ROWS, 128), BF16),
            pltpu.VMEM((EDGE - 1, ROWS, 128), BF16),
            pltpu.VMEM((PIECES, EDGE, SUB, 128), narrow_y),
            pltpu.VMEM((EDGE - 1, PIECES, SUB, 128), narrow_y),
            pltpu.VMEM((PIECES, SUB, 128), narrow_z),
            pltpu.VMEM((EDGE - 1, PIECES, SUB, 128), narrow_z),
            pltpu.VMEM((PIECES, EDGE, SUB, 128), BF16),
            pltpu.VMEM((TILES, ROWS, 128), BF16),
        ]

    updated, energy, force = pl.pallas_call(
        block_kernel,
        name="block",
        out_shape=(
            jax.ShapeDtypeStruct((ATOMS, CHANNELS), BF16),
            jax.ShapeDtypeStruct((1, ATOMS), F32),
            jax.ShapeDtypeStruct((3, 1, ATOMS), F32),
        ),
        in_specs=[pl.BlockSpec(memory_space=pltpu.SMEM)] + [hbm] * 10,
        out_specs=(vmem, vmem, vmem),
        scratch_shapes=[
            pltpu.VMEM((ATOMS, CHANNELS), BF16),
            pltpu.VMEM((3, 1, ATOMS), F32),
            pltpu.VMEM((BASES, CHANNELS, CHANNELS), BF16),
            pltpu.VMEM((CHANNELS, CHANNELS), BF16),
            pltpu.VMEM((64, CHANNELS), BF16),
            pltpu.VMEM((64, CHANNELS), BF16),
            pltpu.VMEM((1, 64), F32),
            pltpu.VMEM((1, CHANNELS), F32),
            pltpu.VMEM((64, WAVES), F32),
            pltpu.VMEM((3, WAVES), jnp.int32),
            pltpu.VMEM((27, ATOMS + 16, CHANNELS), BF16),
            pltpu.VMEM((27, ATOMS, CHANNELS), BF16),
            pltpu.VMEM((16, ATOMS), F32),
            pltpu.VMEM((6, 8, ATOMS), F32),
            pltpu.VMEM((8, 128), F32),
            pltpu.VMEM((TILES, ROWS, 256), F32),
            pltpu.VMEM((TILES, ROWS, 256), BF16),
            pltpu.VMEM((TILES, ROWS, 256), BF16),
            pltpu.VMEM((TILES, ROWS, 128), F32),
            pltpu.VMEM((TILES, ROWS, 128), BF16),
            pltpu.VMEM((TILES, ROWS, 128), BF16),
        ]
        + reduce_buffers(BF16, BF16)
        + reduce_buffers(BF16, BF16)
        + [
            pltpu.VMEM((3, ATOMS, ATOMS), F32),
            pltpu.VMEM((ATOMS, 3 * BASES * ATOMS), BF16),
            pltpu.VMEM((CHANNELS, BASES * CHANNELS), BF16),
            pltpu.VMEM((27, BASES * ATOMS, CHANNELS), BF16),
            pltpu.VMEM((BASES * ATOMS, CHANNELS), F32),
            pltpu.VMEM((BASES * ATOMS, 3 * 128), F32),
            pltpu.VMEM((BASES * ATOMS, 2 * CHANNELS), BF16),
            pltpu.VMEM((256, 256), F32),
            dma((10,)),
            dma((2, 5, PIECES, EDGE - 1)),
            dma((2, 5, PIECES, EDGE - 1)),
            dma((2, 5, 2)),
            dma((2, 5, 2)),
        ],
        compiler_params=pltpu.CompilerParams(
            collective_id=0, has_side_effects=True, vmem_limit_bytes=48 * 1024 * 1024
        ),
    )(
        counts.reshape(1),
        pltpu.with_memory_space_constraint(features[0, 0, 0], pltpu.HBM),
        pltpu.with_memory_space_constraint(positions.reshape(3, 1, ATOMS), pltpu.HBM),
        pltpu.with_memory_space_constraint(w_proj, pltpu.HBM),
        pltpu.with_memory_space_constraint(w_mix, pltpu.HBM),
        pltpu.with_memory_space_constraint(w_long, pltpu.HBM),
        pltpu.with_memory_space_constraint(w_charge, pltpu.HBM),
        pltpu.with_memory_space_constraint(charge_bias.reshape(1, 64), pltpu.HBM),
        pltpu.with_memory_space_constraint(w_energy.reshape(1, CHANNELS), pltpu.HBM),
        pltpu.with_memory_space_constraint(k_filter, pltpu.HBM),
        pltpu.with_memory_space_constraint(k_index, pltpu.HBM),
    )
    return (
        updated[None, None, None],
        energy.reshape(1, 1, 1, ATOMS),
        force.reshape(1, 1, 1, 3, ATOMS),
    )


def solution(mesh):
    cells = P("gx", "gy", "gz")
    in_specs = (cells, cells, cells) + (P(),) * 8
    return jax.shard_map(
        shards, mesh=mesh, in_specs=in_specs, out_specs=(cells, cells, cells), check_vma=False
    )
```
